128 devices in a mesh: dp: 8 (over y, core), expert: 16 (over z, x).
Axes of the slice: x: 4, y: 4, z: 4, core: 2. Of those that a mesh axis runs over, the one named last changes fastest.
Arguments:
- tokens: bfloat16 [16384, 3584], P(('dp', 'expert')), may hold values from -24 to 24
- cotangent: bfloat16 [16384, 3584], P(('dp', 'expert')), may hold values from -1.5 to 1.5
- gates: bfloat16 [16384, 2], P(('dp', 'expert')), may hold values from 0.19921875 to 1
- expert_ids: int32 [16384, 2], P(('dp', 'expert')), may hold values from 0 to 15, all different within a row; in each aligned block of 128 rows (0 to 127, 128 to 255, ...) at most 24 rows name the same one
- gate_w: bfloat16 [16, 3584, 1024], P('expert'), may hold values from -0.09375 to 0.09375
- up_w: bfloat16 [16, 3584, 1024], P('expert'), may hold values from -0.09375 to 0.09375
- down_w: bfloat16 [16, 1024, 3584], P('expert'), may hold values from -0.1875 to 0.1875
Outputs:
- grad_tokens: bfloat16 [16384, 3584], P('dp', 'expert')
- grad_gate_w: bfloat16 [16, 3584, 1024], P('expert', 'dp')
- grad_up_w: bfloat16 [16, 3584, 1024], P('expert', 'dp')
- grad_gates: bfloat16 [16384, 2], P(('dp', 'expert'))
The draws below stay inside these ranges and needn't reach their ends.
Inputs may be any that keep to these rules, and one draw needn't show every extreme that they name: `expert_ids`: each token names 2 different experts; among the 128 tokens of one device no expert is named more than 24 times, and in every draw some expert is named exactly 24 times by some device's tokens.
All inputs are finite; a program needn't handle non-finite values.
Results may differ from the reference program's by a relative error of at most 0.014.
Values may be sent and summed in bfloat16 or wider, within the bound.
A program may use at most 192 MiB of HBM per device.

```python
import math
import jax
import jax.numpy as jnp
import numpy as np
from jax import lax

D = 3584
H = 1024
TOP = 2
TOK_DEV = 128
EXPERTS = 16
CAP = 24
TOKENS = 16384
N_DP = 8
N_EXPERT = 16


def strengthened(array, own_key, source, target, parts, factor):
    def block_of(axis_at):
        return (jnp.arange(array.shape[axis_at]) // (array.shape[axis_at] // parts)).reshape((-1,) + (1,) * (array.ndim - 1 - axis_at))

    first = jax.random.permutation(own_key, parts)[block_of(target)]
    other_side = (block_of(target) + parts // 2) % parts
    return jnp.where((block_of(source) == first) | (block_of(source) == other_side), factor * array, array)


def level_of(own_key, dims, split, low, high):
    def one(axis_at, parts):
        heights = jax.random.uniform(jax.random.fold_in(jax.random.fold_in(own_key, 6), axis_at), (parts,), jnp.float32, low / len(split), high / len(split))
        return jnp.repeat(jnp.exp(heights), dims[axis_at] // parts).reshape((-1,) + (1,) * (len(dims) - axis_at - 1))

    factor_of = one(*split[0])
    for cut in split[1:]:
        factor_of = factor_of * one(*cut)
    return factor_of


def deal_out(rng, own, number, rows, amount, top, limit, lean):
    order = jax.random.permutation(rng, amount)
    heavy_load, common = portions_of(amount, rows * top, limit, lean, True), portions_of(amount, rows * top, limit, lean, False)
    places = jnp.arange(amount)

    def named(sizes, rotation):
        used = int((sizes > 0).sum())
        fixed = max(1, used // 4)
        passed = fixed + (places - fixed + rotation * (used - fixed)) % max(1, amount - fixed)
        return jnp.zeros((amount,), jnp.int32).at[order[jnp.where(places < fixed, places, passed)]].set(jnp.asarray(sizes, jnp.int32))

    sizes = jnp.where(number % 4 == 0, named(heavy_load, number // 4), named(common, number - number // 4 - 1))
    mixed = jax.random.permutation(jax.random.fold_in(own, 3), amount)
    source_of, receiver = mixed[0:amount // 2 * 2:2], mixed[1:amount // 2 * 2:2]
    margin = jnp.minimum(sizes[source_of] - 1, limit - sizes[receiver]) // 2
    margin = jnp.where((source_of == order[0]) | (receiver == order[0]) | (sizes[receiver] == 0), 0, jnp.maximum(margin, 0))
    passed = jax.random.randint(jax.random.fold_in(own, 4), (amount // 2,), 0, 1 << 20) % (margin + 1)
    sizes = sizes.at[source_of].add(-passed).at[receiver].add(passed)
    items = jnp.searchsorted(jnp.cumsum(sizes), jnp.arange(rows * top), side="right").astype(jnp.int32)
    listing = items.reshape(top, rows).T
    listing = listing[jax.random.permutation(jax.random.fold_in(own, 1), rows)]
    rotation = jax.random.randint(jax.random.fold_in(own, 2), (rows, 1), 0, top)
    return jnp.take_along_axis(listing, (jnp.arange(top)[None, :] + rotation) % top, axis=1)


def portions_of(number_of, total, bound, lean, full):
    loads = [(1 << 20) // math.isqrt(rank ** lean) + 1 for rank in range(1, number_of + 1)]
    largest = bound if full else min(bound, max(-(-total // number_of), total * loads[0] // sum(loads)))
    least = 1 if total - largest >= number_of - 1 else 0
    holding, surplus = [largest] + [least] * (number_of - 1), total - largest - least * (number_of - 1)
    while surplus > 0:
        free = [i for i in range(1, number_of) if holding[i] < largest] or [i for i in range(1, number_of) if holding[i] < bound]
        mass, remaining = sum([loads[i] for i in free]), surplus
        for i in free:
            addition = min(bound - holding[i], max(1, remaining * loads[i] // mass), surplus)
            holding[i] = holding[i] + addition
            surplus = surplus - addition
    return np.array(holding)


def centred(key, shape, deviation, reach, cuts=(), kind=jnp.bfloat16):
    factor_of = level_of(key, shape, cuts, -0.22, 0.18) if cuts else 1.0
    array = jax.random.normal(key, shape, jnp.float32) * deviation * factor_of
    return jnp.minimum(jnp.maximum(array, -reach), reach).astype(kind)


def bell_draw_with(key, dims, spread, limit, shards, heavy, kind=jnp.bfloat16):
    drawn = spread * jax.random.normal(key, dims, jnp.float32)
    if shards:
        drawn = drawn * level_of(key, dims, shards, -0.22, 0.18)
    return jnp.clip(strengthened(drawn, jax.random.fold_in(key, 3), *heavy), -limit, limit).astype(kind)


def setup_inputs(seed: int = 0) -> dict:
    splits = jax.random.split(jax.random.key(seed), 8)
    tokens = bell_draw_with(splits[0], (TOKENS, D), 1.0, 24.0, ((0, 128),), (0, 1, 128, 5.5))
    cotangent = centred(splits[1], (TOKENS, D), 0.25, 1.5, ((0, 128),))
    gates = jnp.clip(jnp.exp(math.log(1.0) - 1.6133518 * jax.random.uniform(splits[2], (TOKENS, TOP), jnp.float32) ** level_of(splits[2], (TOKENS, TOP), ((0, 128),), -0.2, 0.2)), 0.19921875, 1.0).astype(jnp.bfloat16)
    expert_ids_keys = jax.random.split(jax.random.fold_in(splits[3], 1), TOKENS // TOK_DEV)
    expert_ids_turns = jax.random.permutation(jax.random.fold_in(splits[3], 3), TOKENS // TOK_DEV)
    expert_ids = jax.vmap(lambda own, number: deal_out(jax.random.fold_in(splits[3], 2), own, number, TOK_DEV, EXPERTS, TOP, CAP, 2))(expert_ids_keys, expert_ids_turns).reshape((TOKENS, TOP))
    gate_w = centred(splits[4], (EXPERTS, D, H), D ** -0.5, 0.09375, ((0, 16),))
    up_w = centred(splits[5], (EXPERTS, D, H), D ** -0.5, 0.09375, ((0, 16),))
    down_w = centred(splits[6], (EXPERTS, H, D), H ** -0.5, 0.1875, ((0, 16),))
    return dict(tokens=tokens, cotangent=cotangent, gates=gates, expert_ids=expert_ids, gate_w=gate_w, up_w=up_w, down_w=down_w)


def reference(tokens, cotangent, gates, expert_ids, gate_w, up_w, down_w):
    slots_dev = TOK_DEV * TOP
    blocks = N_DP * N_EXPERT
    sentinel = TOKENS * TOP
    ids_block = expert_ids.reshape(blocks, slots_dev)
    onehot = (ids_block[:, :, None] == jnp.arange(EXPERTS, dtype=jnp.int32)[None, None, :]).astype(jnp.int32)
    position = jnp.sum(jnp.cumsum(onehot, axis=1) * onehot, axis=2) - 1
    block_id = jnp.arange(blocks, dtype=jnp.int32)[:, None]
    group_id = block_id // N_EXPERT
    source_id = block_id % N_EXPERT
    target = ((group_id * EXPERTS + ids_block) * N_EXPERT + source_id) * CAP + position
    flat_slot = jnp.arange(sentinel, dtype=jnp.int32).reshape(blocks, slots_dev)
    slot_map = jnp.full((N_DP * EXPERTS * N_EXPERT * CAP,), sentinel, jnp.int32)
    slot_map = slot_map.at[target.reshape(-1)].set(flat_slot.reshape(-1))
    slot_map = slot_map.reshape(N_DP, EXPERTS, N_EXPERT * CAP).transpose(1, 0, 2)
    tokens_ext = jnp.concatenate([tokens, jnp.zeros((1, D), tokens.dtype)], axis=0)
    cot_ext = jnp.concatenate([cotangent, jnp.zeros((1, D), cotangent.dtype)], axis=0)
    gates_ext = jnp.concatenate([gates.reshape(-1), jnp.zeros((1,), gates.dtype)], axis=0)

    def expert_step(running, inputs):
        slot_dx, slot_dg = running
        slot_index, gate_mat, up_mat, down_mat = inputs
        flat_index = slot_index.reshape(-1)
        row_token = jnp.where(flat_index == sentinel, TOKENS, flat_index // TOP)
        token_rows = tokens_ext[row_token]
        grad_rows = cot_ext[row_token]
        row_gates = gates_ext[flat_index].astype(jnp.float32)
        gate_pre = jnp.dot(token_rows, gate_mat, preferred_element_type=jnp.float32)
        up_pre = jnp.dot(token_rows, up_mat, preferred_element_type=jnp.float32)
        sigmoid_a = jax.nn.sigmoid(gate_pre)
        silu_a = gate_pre * sigmoid_a
        hidden = (silu_a * up_pre).astype(jnp.bfloat16)
        back = jnp.dot(grad_rows, down_mat.T, preferred_element_type=jnp.float32)
        gate_score = jnp.sum(back * hidden.astype(jnp.float32), axis=1).astype(jnp.bfloat16)
        hidden_grad = back * row_gates[:, None]
        gate_grad = (hidden_grad * up_pre * sigmoid_a * (1.0 + gate_pre * (1.0 - sigmoid_a))).astype(jnp.bfloat16)
        up_grad = (hidden_grad * silu_a).astype(jnp.bfloat16)
        row_grad = (jnp.dot(gate_grad, gate_mat.T, preferred_element_type=jnp.float32)
                    + jnp.dot(up_grad, up_mat.T, preferred_element_type=jnp.float32)).astype(jnp.bfloat16)
        grouped_x = token_rows.reshape(N_DP, -1, D).astype(jnp.float32)
        part_g = jnp.einsum('gmd,gmh->gdh', grouped_x, gate_grad.reshape(N_DP, -1, H).astype(jnp.float32))
        part_u = jnp.einsum('gmd,gmh->gdh', grouped_x, up_grad.reshape(N_DP, -1, H).astype(jnp.float32))
        part_g = lax.optimization_barrier(part_g.astype(jnp.bfloat16)).astype(jnp.float32)
        part_u = lax.optimization_barrier(part_u.astype(jnp.bfloat16)).astype(jnp.float32)
        grad_g = (jnp.sum(part_g, axis=0) * (1.0 / N_DP)).astype(jnp.bfloat16)
        grad_u = (jnp.sum(part_u, axis=0) * (1.0 / N_DP)).astype(jnp.bfloat16)
        slot_dx = slot_dx.at[flat_index].set(row_grad)
        slot_dg = slot_dg.at[flat_index].set(gate_score)
        return (slot_dx, slot_dg), (grad_g, grad_u)

    start_dx = jnp.zeros((sentinel + 1, D), jnp.bfloat16)
    start_dg = jnp.zeros((sentinel + 1,), jnp.bfloat16)
    (slot_dx, slot_dg), (grad_gate_w, grad_up_w) = lax.scan(
        expert_step, (start_dx, start_dg), (slot_map, gate_w, up_w, down_w))
    grad_tokens = jnp.sum(slot_dx[:sentinel].reshape(TOKENS, TOP, D).astype(jnp.float32), axis=1).astype(jnp.bfloat16)
    grad_gates = slot_dg[:sentinel].reshape(TOKENS, TOP)
    return (grad_tokens, grad_gate_w, grad_up_w, grad_gates)
```

```python
import functools
import jax
import jax.numpy as jnp
from jax import lax
from jax.experimental import pallas as pl
from jax.experimental.pallas import tpu as pltpu
from jax.sharding import PartitionSpec as P

MESH = pl.DeviceIdType.MESH
BF = jnp.bfloat16
F32 = jnp.float32
LANES = 128


def grid_of(count):
    side = 1
    while side * side * 4 <= count:
        side *= 2
    return count // side, side


def dot_nt(left, right):
    return lax.dot_general(left, right, (((1,), (1,)), ((), ())), preferred_element_type=F32)


def kernel(
    n_dp,
    n_ex,
    cap,
    ids_ref,
    gts_ref,
    x_ref,
    y_ref,
    wg_hbm,
    wu_hbm,
    wd_hbm,
    gt_ref,
    gg_hbm,
    gu_hbm,
    gs_ref,
    wg,
    wu,
    wd,
    tgt,
    sx,
    sy,
    rx,
    ry,
    xt,
    av,
    bv,
    d2,
    score,
    ssend,
    sret,
    rg,
    rr,
    gath,
    xtg,
    dg,
    wo,
    wsem,
    tsend,
    trecv,
    xsend,
    xrecv,
    ysend,
    yrecv,
    psend,
    precv,
    qsend,
    dsend,
    drecv,
    dloc,
    rsend,
    rrecv,
    csend,
    crecv,
    osend,
    orecv,
    oloc,
    lsem,
):
    n_z, n_x = grid_of(n_ex)
    n_y = n_dp // 2
    tok, width = x_ref.shape
    hid = wg.shape[1]
    rows = n_ex * cap
    feat = width // n_ex
    deep = width // n_y
    half = deep // 2
    tile = min(256, hid)
    n_t = hid // tile
    me_e = lax.axis_index("expert")
    me_d = lax.axis_index("dp")
    pos_z, pos_x = me_e // n_x, me_e % n_x
    pos_y, core = me_d // 2, me_d % 2
    other = me_d + 1 - 2 * core

    def at(o):
        return ((pos_z + o // n_x) % n_z) * n_x + (pos_x + o % n_x) % n_x

    def copy_to(src, dst, send, recv, dp_id, ex_id):
        return pltpu.make_async_remote_copy(
            src_ref=src,
            dst_ref=dst,
            send_sem=send,
            recv_sem=recv,
            device_id=(dp_id, ex_id),
            device_id_type=MESH,
        )

    def slab(o):
        return pl.ds(o * (cap // 8), cap // 8)

    sx2, rx2 = sx.reshape(rows, width), rx.reshape(rows, width)
    sy2, ry2 = sy.reshape(rows, width + LANES), ry.reshape(rows, width + LANES)
    ssend2, sret2 = ssend.reshape(rows, LANES), sret.reshape(rows, LANES)

    def tiles(i):
        return pl.ds(pl.multiple_of(i * tile, tile), tile)

    loads = [
        pltpu.make_async_copy(wg_hbm, wg, wsem.at[0]),
        pltpu.make_async_copy(wu_hbm, wu, wsem.at[1]),
        pltpu.make_async_copy(wd_hbm, wd, wsem.at[2]),
    ]
    for load in loads:
        load.start()

    barrier = pltpu.get_barrier_semaphore()

    @pl.loop(1, n_ex)
    def _(o):
        pl.semaphore_signal(barrier, inc=1, device_id=(me_d, at(o)), device_id_type=MESH)

    @pl.loop(1, n_dp)
    def _(o):
        pl.semaphore_signal(
            barrier, inc=1, device_id=((me_d + o) % n_dp, me_e), device_id_type=MESH
        )

    ids = ids_ref[...]
    expert_no = lax.broadcasted_iota(jnp.int32, (n_ex, tok), 0)
    named = [(expert_no == ids[k : k + 1, :]).astype(F32) for k in range(2)]
    before = (
        lax.broadcasted_iota(jnp.int32, (tok, tok), 0)
        < lax.broadcasted_iota(jnp.int32, (tok, tok), 1)
    ).astype(F32)
    count = jnp.dot(
        (named[0] + named[1]).astype(BF), before.astype(BF), preferred_element_type=F32
    )
    place = [
        jnp.sum(named[k] * count, axis=0, keepdims=True) + (ids[k : k + 1, :] * cap).astype(F32)
        for k in range(2)
    ]
    slot_no = lax.broadcasted_iota(jnp.int32, (rows, tok), 0).astype(F32)
    picks = [(slot_no == place[k]).astype(F32) for k in range(2)]
    pick = (picks[0] + picks[1]).astype(BF)
    weight = jnp.sum(picks[0] * gts_ref[0:1, :] + picks[1] * gts_ref[1:2, :], axis=1, keepdims=True)
    row_no = lax.broadcasted_iota(jnp.int32, (8, tok), 0)
    tgt[me_e] = jnp.where(row_no == 0, place[0], place[1])

    pl.semaphore_wait(barrier, n_ex - 1 + n_dp - 1)

    def send_x(o):
        e = at(o)
        return copy_to(sx.at[slab(e)], rx.at[slab(o)], xsend.at[o], xrecv.at[o], me_d, e)

    def send_y(o):
        e = at(o)
        return copy_to(sy.at[slab(e)], ry.at[slab(o)], ysend.at[o], yrecv.at[o], me_d, e)

    def send_t(o):
        return copy_to(tgt.at[me_e], tgt.at[me_e], tsend.at[o], trecv.at[o], me_d, at(o))

    block = min(512, width)
    for i in range(width // block):
        span = slice(i * block, (i + 1) * block)
        sx2[:, span] = jnp.dot(pick, x_ref[:, span], preferred_element_type=F32).astype(BF)

    @pl.loop(1, n_ex)
    def _(o):
        send_x(o).start()
        send_t(o).start()

    own_x = pltpu.make_async_copy(sx.at[slab(me_e)], rx.at[slab(0)], lsem.at[0])
    own_x.start()
    for i in range(width // block):
        span = slice(i * block, (i + 1) * block)
        sy2[:, span] = jnp.dot(pick, y_ref[:, span], preferred_element_type=F32).astype(BF)
    sy2[:, width:] = jnp.broadcast_to(weight, (rows, LANES)).astype(BF)
    own_y = pltpu.make_async_copy(sy.at[slab(me_e)], ry.at[slab(0)], lsem.at[1])
    own_y.start()

    @pl.loop(1, n_ex)
    def _(o):
        send_x(o).wait_send()
        send_y(o).start()

    own_x.wait()

    @pl.loop(1, n_ex)
    def _(o):
        send_x(o).wait_recv()

    def send_p(r):
        chip = (pos_y + r) % n_y
        return copy_to(
            xt.at[pl.ds(pl.multiple_of(chip * deep, deep), deep)],
            xtg.at[me_d],
            psend.at[r],
            precv.at[me_d],
            chip * 2 + core,
            me_e,
        )

    def turn(r):
        chip = (pos_y + r) % n_y

        @pl.loop(0, deep // LANES)
        def _(i):
            start = pl.multiple_of(chip * deep + i * LANES, LANES)
            xt[pl.ds(start, LANES), :] = rx2[:, pl.ds(start, LANES)].T

    for r in [n_y // 2] + [r for r in range(1, n_y) if r != n_y // 2]:
        turn(r)
        send_p(r).start()
    turn(0)
    home = pl.ds(pl.multiple_of(pos_y * deep, deep), deep)
    own_p = pltpu.make_async_copy(xt.at[home], xtg.at[me_d], lsem.at[2])
    own_p.start()
    give_own = copy_to(xt.at[home], xtg.at[me_d], qsend.at[0], precv.at[me_d], other, me_e)
    give_own.start()

    loads[0].wait()
    loads[1].wait()

    @pl.loop(0, n_t)
    def _(i):
        av[:, tiles(i)] = jnp.dot(rx2[...], wg[:, tiles(i)], preferred_element_type=F32)
        bv[:, tiles(i)] = jnp.dot(rx2[...], wu[:, tiles(i)], preferred_element_type=F32)

    def relay(r):
        g = ((pos_y + n_y - r) % n_y) * 2 + core
        return copy_to(xtg.at[g], xtg.at[g], qsend.at[r], precv.at[g], other, me_e)

    @pl.loop(1, n_y)
    def _(r):
        relay(r).wait_recv()
        relay(r).start()

    own_y.wait()

    @pl.loop(1, n_ex)
    def _(o):
        send_y(o).wait_recv()

    loads[2].wait()
    score[...] = jnp.zeros_like(score)
    mine = pl.ds(pl.multiple_of(me_d * rows, rows), rows)

    def send_d(r, which, i):
        side = core if which == 0 else 1 - core
        chip = (pos_y + r) % n_y
        return copy_to(
            d2.at[side, :, tiles(i)],
            dg.at[mine, tiles(i)],
            dsend.at[(r * 2 + which) * n_t + i],
            drecv.at[me_d * n_t + i],
            chip * 2 + side,
            me_e,
        )

    def keep_d(i):
        return pltpu.make_async_copy(d2.at[core, :, tiles(i)], dg.at[mine, tiles(i)], dloc.at[i])

    @pl.loop(0, n_t)
    def _(i):
        back = dot_nt(ry2[:, :width], wd[tiles(i), :])
        a = av[:, tiles(i)]
        b = bv[:, tiles(i)]
        w = jnp.tile(ry2[:, width:].astype(F32), (1, tile // LANES))
        sig = jax.nn.sigmoid(a)
        silu = a * sig
        hidden = (silu * b).astype(BF)
        part = back * hidden.astype(F32)
        total = part[:, :LANES]
        for k in range(1, tile // LANES):
            total = total + part[:, k * LANES : (k + 1) * LANES]
        score[...] += total
        grad = back * w
        d2[0, :, tiles(i)] = (grad * b * sig * (1.0 + a * (1.0 - sig))).astype(BF)
        d2[1, :, tiles(i)] = (grad * silu).astype(BF)
        for r in [n_y // 2] + [r for r in range(1, n_y) if r != n_y // 2]:
            send_d(r, 0, i).start()
            send_d(r, 1, i).start()
        send_d(0, 1, i).start()
        keep_d(i).start()

    ssend2[...] = jnp.broadcast_to(jnp.sum(score[...], axis=1, keepdims=True), (rows, LANES)).astype(BF)

    def send_c(o):
        e = ((pos_z + n_z - o // n_x) % n_z) * n_x + (pos_x + n_x - o % n_x) % n_x
        return copy_to(ssend.at[slab(o)], sret.at[slab(me_e)], csend.at[o], crecv.at[o], me_d, e)

    @pl.loop(1, n_ex)
    def _(o):
        send_c(o).start()

    own_c = pltpu.make_async_copy(ssend.at[slab(0)], sret.at[slab(me_e)], lsem.at[3])
    own_c.start()

    def send_r(o):
        return copy_to(rg.at[o], rr.at[me_e], rsend.at[o], rrecv.at[o], me_d, at(o))

    own_r = pltpu.make_async_copy(rg.at[0], rr.at[me_e], lsem.at[4])

    def block_grad(o):
        span = pl.ds(pl.multiple_of(at(o) * feat, feat), feat)
        rg[o] = (dot_nt(d2[0], wg[span, :]) + dot_nt(d2[1], wu[span, :])).astype(BF)

    @pl.loop(1, n_ex)
    def _(o):
        block_grad(o)
        send_r(o).start()

    block_grad(0)
    own_r.start()

    @pl.loop(1, n_ex)
    def _(o):
        send_t(o).wait_recv()

    own_r.wait()

    @pl.loop(1, n_ex)
    def _(o):
        send_r(o).wait_recv()

    lane_no = lax.broadcasted_iota(jnp.int32, (tok, rows), 1).astype(F32)
    for s in range(n_ex):
        sz, sx_ = s // n_x, s % n_x
        column = tgt[s].T
        hit = (lane_no == column[:, 0:1]) | (lane_no == column[:, 1:2])
        choose = hit.astype(F32).astype(BF)
        for e in range(n_ex):
            o = ((e // n_x - sz) % n_z) * n_x + (e % n_x - sx_) % n_x
            gath[e * cap : (e + 1) * cap, :] = rr[e, o * cap : (o + 1) * cap, :]
        gt_ref[s * tok : (s + 1) * tok, :] = jnp.dot(
            choose, gath[...], preferred_element_type=F32
        ).astype(BF)

    own_c.wait()

    @pl.loop(1, n_ex)
    def _(o):
        send_c(o).wait_recv()

    column = tgt[me_e].T
    back_scores = sret2[...]
    first = jnp.dot(
        (lane_no == column[:, 0:1]).astype(F32).astype(BF), back_scores, preferred_element_type=F32
    )
    second = jnp.dot(
        (lane_no == column[:, 1:2]).astype(F32).astype(BF), back_scores, preferred_element_type=F32
    )
    which = lax.broadcasted_iota(jnp.int32, (tok, LANES), 1)
    gs_ref[...] = jnp.where(which == 0, first, second).astype(BF)[:, :2]

    own_p.wait()

    @pl.loop(0, n_y)
    def _(r):
        g = ((pos_y + r) % n_y) * 2 + 1 - core
        copy_to(xtg.at[g], xtg.at[g], qsend.at[0], precv.at[g], other, me_e).wait_recv()

    def own_half(i, out):
        return pltpu.make_async_copy(wo.at[core, :, tiles(i)], out.at[:, tiles(i)], oloc.at[i])

    def other_half(i, out):
        return copy_to(
            wo.at[1 - core, :, tiles(i)],
            out.at[:, tiles(i)],
            osend.at[i],
            orecv.at[i],
            other,
            me_e,
        )

    @pl.loop(0, n_t)
    def _(i):
        keep_d(i).wait()

        @pl.loop(1, n_dp)
        def _(r):
            g = (me_d + r) % n_dp
            there = pl.ds(pl.multiple_of(g * rows, rows), rows)
            copy_to(
                dg.at[there, tiles(i)],
                dg.at[there, tiles(i)],
                dsend.at[0],
                drecv.at[g * n_t + i],
                other,
                me_e,
            ).wait_recv()

        for h in range(2):
            acc = jnp.zeros((half, tile), F32)
            for g in range(n_dp):
                acc = acc + jnp.dot(
                    xtg[g, h * half : (h + 1) * half, :],
                    dg[g * rows : (g + 1) * rows, tiles(i)],
                    preferred_element_type=F32,
                )
            wo[h, :, tiles(i)] = (acc * (1.0 / n_dp)).astype(BF)

        @pl.when(core == 0)
        def _():
            own_half(i, gg_hbm).start()
            other_half(i, gg_hbm).start()

        @pl.when(core == 1)
        def _():
            own_half(i, gu_hbm).start()
            other_half(i, gu_hbm).start()

    @pl.loop(0, n_t)
    def _(i):
        own_half(i, gg_hbm).wait()
        other_half(i, gg_hbm).wait()

    @pl.loop(1, n_ex)
    def _(o):
        send_t(o).wait_send()
        send_y(o).wait_send()
        send_c(o).wait_send()
        send_r(o).wait_send()

    give_own.wait_send()

    @pl.loop(1, n_y)
    def _(r):
        send_p(r).wait_send()
        relay(r).wait_send()

    @pl.loop(0, n_t)
    def _(i):
        send_d(0, 1, i).wait_send()

        @pl.loop(1, n_y)
        def _(r):
            send_d(r, 0, i).wait_send()
            send_d(r, 1, i).wait_send()


def local(tokens, cotangent, gates, expert_ids, gate_w, up_w, down_w):
    tok, width = tokens.shape
    top = expert_ids.shape[1]
    n_ex = lax.axis_size("expert")
    n_dp = lax.axis_size("dp")
    cap = 3 * tok * top // (2 * n_ex)
    hid = gate_w.shape[2]
    rows = n_ex * cap
    feat = width // n_ex
    n_y = n_dp // 2
    deep = width // n_y
    n_t = hid // min(256, hid)
    vmem = pl.BlockSpec(memory_space=pltpu.VMEM)
    hbm = pl.BlockSpec(memory_space=pl.ANY)
    dma = pltpu.SemaphoreType.DMA
    scratch = [
        pltpu.VMEM((width, hid), BF),
        pltpu.VMEM((width, hid), BF),
        pltpu.VMEM((hid, width), BF),
        pltpu.VMEM((n_ex, 8, tok), F32),
        pltpu.VMEM((rows // 8, 8, width), BF),
        pltpu.VMEM((rows // 8, 8, width + LANES), BF),
        pltpu.VMEM((rows // 8, 8, width), BF),
        pltpu.VMEM((rows // 8, 8, width + LANES), BF),
        pltpu.VMEM((width, rows), BF),
        pltpu.VMEM((rows, hid), F32),
        pltpu.VMEM((rows, hid), F32),
        pltpu.VMEM((2, rows, hid), BF),
        pltpu.VMEM((rows, LANES), F32),
        pltpu.VMEM((rows // 8, 8, LANES), BF),
        pltpu.VMEM((rows // 8, 8, LANES), BF),
        pltpu.VMEM((n_ex, rows, feat), BF),
        pltpu.VMEM((n_ex, rows, feat), BF),
        pltpu.VMEM((rows, feat), BF),
        pltpu.VMEM((n_dp, deep, rows), BF),
        pltpu.VMEM((n_dp * rows, hid), BF),
        pltpu.VMEM((2, deep // 2, hid), BF),
        dma((3,)),
        dma((n_ex,)),
        dma((n_ex,)),
        dma((n_ex,)),
        dma((n_ex,)),
        dma((n_ex,)),
        dma((n_ex,)),
        dma((n_y,)),
        dma((n_dp,)),
        dma((n_y,)),
        dma((2 * n_y * n_t,)),
        dma((n_dp * n_t,)),
        dma((n_t,)),
        dma((n_ex,)),
        dma((n_ex,)),
        dma((n_ex,)),
        dma((n_ex,)),
        dma((n_t,)),
        dma((n_t,)),
        dma((n_t,)),
        dma((5,)),
    ]
    return pl.pallas_call(
        functools.partial(kernel, n_dp, n_ex, cap),
        out_shape=(
            jax.ShapeDtypeStruct((n_ex * tok, feat), BF),
            jax.ShapeDtypeStruct((width // n_dp, hid), BF),
            jax.ShapeDtypeStruct((width // n_dp, hid), BF),
            jax.ShapeDtypeStruct((tok, top), BF),
        ),
        in_specs=[vmem, vmem, vmem, vmem, hbm, hbm, hbm],
        out_specs=(vmem, hbm, hbm, vmem),
        scratch_shapes=scratch,
        compiler_params=pltpu.CompilerParams(
            collective_id=0, has_side_effects=True, vmem_limit_bytes=64 * 1024 * 1024
        ),
    )(
        expert_ids.T,
        gates.astype(F32).T,
        tokens,
        cotangent,
        gate_w[0],
        up_w[0],
        down_w[0],
    )


def shard(tokens, cotangent, gates, expert_ids, gate_w, up_w, down_w):
    grad_tokens, grad_gate, grad_up, grad_gates = local(
        tokens, cotangent, gates, expert_ids, gate_w, up_w, down_w
    )
    return grad_tokens, grad_gate[None], grad_up[None], grad_gates


def solution(mesh):
    placed = (
        P(("dp", "expert"), None),
        P(("dp", "expert"), None),
        P(("dp", "expert"), None),
        P(("dp", "expert"), None),
        P("expert", None, None),
        P("expert", None, None),
        P("expert", None, None),
    )
    return jax.shard_map(
        shard,
        mesh=mesh,
        in_specs=placed,
        out_specs=(
            P("dp", "expert"),
            P("expert", "dp", None),
            P("expert", "dp", None),
            P(("dp", "expert"), None),
        ),
        check_vma=False,
    )
```

```python
import functools
import jax
import jax.numpy as jnp
from jax import lax
from jax.experimental import pallas as pl
from jax.experimental.pallas import tpu as pltpu
from jax.sharding import PartitionSpec as P

MESH = pl.DeviceIdType.MESH
BF = jnp.bfloat16
F32 = jnp.float32
LANES = 128


def grid_of(count):
    side = 1
    while side * side * 4 <= count:
        side *= 2
    return count // side, side


def dot_nt(left, right):
    return lax.dot_general(left, right, (((1,), (1,)), ((), ())), preferred_element_type=F32)


def kernel(
    n_dp,
    n_ex,
    cap,
    ids_ref,
    gts_ref,
    x_hbm,
    y_hbm,
    wg_hbm,
    wu_hbm,
    wd_hbm,
    gt_ref,
    gg_hbm,
    gu_hbm,
    gs_ref,
    wg,
    wu,
    wd,
    held,
    tgt,
    sx,
    sy,
    rx,
    ry,
    av,
    bv,
    d2,
    score,
    ssend,
    sret,
    rg,
    rr,
    xg,
    dg,
    xtt,
    acc,
    wo,
    wsem,
    tsend,
    trecv,
    xsend,
    xrecv,
    ysend,
    yrecv,
    psend,
    precv,
    qsend,
    dsend,
    drecv,
    fsend,
    dloc,
    rsend,
    rrecv,
    csend,
    crecv,
    osend,
    orecv,
    oloc,
    lsem,
):
    n_z, n_x = grid_of(n_ex)
    n_y = n_dp // 2
    tok, width = held.shape
    hid = wg.shape[1]
    rows = n_ex * cap
    part = rows // 2
    eights = cap // 8
    span8 = part // 8
    feat = width // n_ex
    deep = width // n_y
    half = deep // 2
    tile = hid // 2
    wide = min(256, hid)
    n_w = hid // wide
    me_e = lax.axis_index("expert")
    me_d = lax.axis_index("dp")
    pos_z, pos_x = me_e // n_x, me_e % n_x
    pos_y, core = me_d // 2, me_d % 2
    other = me_d + 1 - 2 * core
    near = sorted({1, n_y - 1})
    hops = [r for r in [n_y // 2] + near if r]
    hops = sorted(set(hops), key=hops.index)

    signs = [(a, b) for b in range(n_x) for a in range(n_z)]
    signs.sort(key=lambda t: (min(t[0], n_z - t[0]) + min(t[1], n_x - t[1]), t))
    order = [t for t in signs if t[0] % 2 == 0] + [t for t in signs if t[0] % 2 == 1]
    size = n_ex // 2

    def to(q):
        return ((pos_z + order[q][0]) % n_z) * n_x + (pos_x + order[q][1]) % n_x

    def source(q):
        return ((pos_z + n_z - order[q][0]) % n_z), (pos_x + n_x - order[q][1]) % n_x

    def copy_to(src, dst, send, recv, dp_id, ex_id):
        return pltpu.make_async_remote_copy(
            src_ref=src,
            dst_ref=dst,
            send_sem=send,
            recv_sem=recv,
            device_id=(dp_id, ex_id),
            device_id_type=MESH,
        )

    def slab(o):
        return pl.ds(o * eights, eights)

    def tiles(i):
        return slice(i * tile, (i + 1) * tile)

    sx2, rx2 = sx.reshape(rows, width), rx.reshape(rows, width)
    sy2, ry2 = sy.reshape(rows, width + LANES), ry.reshape(rows, width + LANES)
    ssend2, sret2 = ssend.reshape(rows, LANES), sret.reshape(rows, LANES)
    xg2 = xg.reshape(2 * n_dp * part, deep)
    rr2 = rr.reshape(n_ex, rows, feat)

    load_x = pltpu.make_async_copy(x_hbm, held, lsem.at[7])
    load_y = pltpu.make_async_copy(y_hbm, held, lsem.at[8])
    load_x.start()
    loads = [
        pltpu.make_async_copy(wg_hbm, wg, wsem.at[0]),
        pltpu.make_async_copy(wu_hbm, wu, wsem.at[1]),
        pltpu.make_async_copy(wd_hbm, wd, wsem.at[2]),
    ]
    for load in loads:
        load.start()

    barrier = pltpu.get_barrier_semaphore()

    @pl.loop(1, n_ex)
    def _(o):
        partner = ((pos_z + o // n_x) % n_z) * n_x + (pos_x + o % n_x) % n_x
        pl.semaphore_signal(barrier, inc=1, device_id=(me_d, partner), device_id_type=MESH)

    @pl.loop(1, n_dp)
    def _(o):
        pl.semaphore_signal(
            barrier, inc=1, device_id=((me_d + o) % n_dp, me_e), device_id_type=MESH
        )

    ids = ids_ref[...]
    expert_no = lax.broadcasted_iota(jnp.int32, (n_ex, tok), 0)
    named = [(expert_no == ids[k : k + 1, :]).astype(F32) for k in range(2)]
    before = (
        lax.broadcasted_iota(jnp.int32, (tok, tok), 0)
        < lax.broadcasted_iota(jnp.int32, (tok, tok), 1)
    ).astype(F32)
    count = jnp.dot(
        (named[0] + named[1]).astype(BF), before.astype(BF), preferred_element_type=F32
    )
    place = [
        jnp.sum(named[k] * count, axis=0, keepdims=True) + (ids[k : k + 1, :] * cap).astype(F32)
        for k in range(2)
    ]
    slot_no = lax.broadcasted_iota(jnp.int32, (rows, tok), 0).astype(F32)
    picks = [(slot_no == place[k]).astype(F32) for k in range(2)]
    pick = (picks[0] + picks[1]).astype(BF)
    gts = gts_ref[...].astype(F32)
    weight = jnp.sum(picks[0] * gts[0:1, :] + picks[1] * gts[1:2, :], axis=1, keepdims=True)
    row_no = lax.broadcasted_iota(jnp.int32, (8, tok), 0)
    tgt[me_e] = jnp.where(row_no == 0, place[0], place[1])

    def send_x(q):
        e = to(q)
        return copy_to(sx.at[slab(e)], rx.at[slab(q)], xsend.at[q], xrecv.at[q], me_d, e)

    def send_y(q):
        e = to(q)
        return copy_to(sy.at[slab(e)], ry.at[slab(q)], ysend.at[q], yrecv.at[q], me_d, e)

    def send_t(q):
        return copy_to(tgt.at[me_e], tgt.at[me_e], tsend.at[q], trecv.at[q], me_d, to(q))

    block = min(512, width)
    load_x.wait()
    for i in range(width // block):
        span = slice(i * block, (i + 1) * block)
        sx2[:, span] = jnp.dot(pick, held[:, span], preferred_element_type=F32).astype(BF)

    load_y.start()
    pl.semaphore_wait(barrier, n_ex - 1 + n_dp - 1)
    for q in range(1, size):
        send_x(q).start()
    own_x = pltpu.make_async_copy(sx.at[slab(me_e)], rx.at[slab(0)], lsem.at[0])
    own_x.start()
    load_y.wait()
    for i in range(width // block):
        span = slice(i * block, (i + 1) * block)
        sy2[:, span] = jnp.dot(pick, held[:, span], preferred_element_type=F32).astype(BF)
    sy2[:, width:] = jnp.broadcast_to(weight, (rows, LANES)).astype(BF)
    for q in range(1, size):
        send_y(q).start()
    own_y = pltpu.make_async_copy(sy.at[slab(me_e)], ry.at[slab(0)], lsem.at[1])
    own_y.start()
    for q in range(size, n_ex):
        send_x(q).start()
    for q in range(size, n_ex):
        send_y(q).start()
    for q in range(1, n_ex):
        send_t(q).start()

    def features(chip):
        return pl.ds(pl.multiple_of(chip * deep, LANES), deep)

    def group8(g):
        return pl.ds(g * span8, span8)

    def send_p(c, r):
        chip = (pos_y + r) % n_y
        return copy_to(
            rx.at[c * span8 : (c + 1) * span8, :, features(chip)],
            xg.at[c, group8(me_d)],
            psend.at[c * n_y + r],
            precv.at[c * n_dp + me_d],
            chip * 2 + core,
            me_e,
        )

    def keep_p(c):
        return pltpu.make_async_copy(
            rx.at[c * span8 : (c + 1) * span8, :, features(pos_y)],
            xg.at[c, group8(me_d)],
            lsem.at[2 + c],
        )

    def give_p(c):
        return copy_to(
            rx.at[c * span8 : (c + 1) * span8, :, features(pos_y)],
            xg.at[c, group8(me_d)],
            qsend.at[c * n_y],
            precv.at[c * n_dp + me_d],
            other,
            me_e,
        )

    def relay_p(c, r):
        g = ((pos_y + n_y - r) % n_y) * 2 + core
        return copy_to(
            xg.at[c, group8(g)],
            xg.at[c, group8(g)],
            qsend.at[c * n_y + r],
            precv.at[c * n_dp + g],
            other,
            me_e,
        )

    def group(g):
        return pl.ds(pl.multiple_of(g * part, 16), part)

    def send_d(c, i, r, which):
        side = core if which == 0 else 1 - core
        chip = (pos_y + r) % n_y
        return copy_to(
            d2.at[c, side, :, tiles(i)],
            dg.at[c, group(me_d), tiles(i)],
            dsend.at[((c * 2 + i) * n_y + r) * 2 + which],
            drecv.at[(c * 2 + i) * n_dp + me_d],
            chip * 2 + side,
            me_e,
        )

    def keep_d(c, i):
        return pltpu.make_async_copy(
            d2.at[c, core, :, tiles(i)], dg.at[c, group(me_d), tiles(i)], dloc.at[c * 2 + i]
        )

    def all_d(c, i):
        return [send_d(c, i, r, which) for r in near for which in (0, 1)] + [send_d(c, i, 0, 1)]

    def forward(c, i, side):
        origin = (pos_y + n_y - 1 + 2 * core) % n_y
        g = origin * 2 + side
        return copy_to(
            dg.at[c, group(g), tiles(i)],
            dg.at[c, group(g), tiles(i)],
            fsend.at[(c * 2 + i) * 2 + side],
            drecv.at[(c * 2 + i) * n_dp + g],
            ((pos_y + n_y + 1 - 2 * core) % n_y) * 2 + core,
            me_e,
        )

    def arrived_d(c, i, g):
        here = dg.at[c, group(g), tiles(i)]
        copy_to(here, here, fsend.at[0], drecv.at[(c * 2 + i) * n_dp + g], other, me_e).wait_recv()

    far = n_y > 2

    def pass_on(c):
        if far:
            for i in range(2):
                for side in range(2):
                    forward(c, i, side).wait_recv()
                    forward(c, i, side).start()

    def forward_stage(c):
        if c == 0:
            own_x.wait()
        for q in range(max(1, c * size), (c + 1) * size):
            send_x(q).wait_recv()
        for r in hops:
            send_p(c, r).start()
        keep_p(c).start()
        give_p(c).start()
        if c == 0:
            loads[0].wait()
            loads[1].wait()
        here = slice(c * part, (c + 1) * part)

        @pl.loop(0, n_w)
        def _(i):
            cols = pl.ds(pl.multiple_of(i * wide, wide), wide)
            av[:, cols] = jnp.dot(rx2[here, :], wg[:, cols], preferred_element_type=F32)
            bv[:, cols] = jnp.dot(rx2[here, :], wu[:, cols], preferred_element_type=F32)

    def hidden_stage(c):
        if c == 0:
            own_y.wait()
            loads[2].wait()
        for q in range(max(1, c * size), (c + 1) * size):
            send_y(q).wait_recv()
        here = slice(c * part, (c + 1) * part)
        score[...] = jnp.zeros_like(score)
        for i in range(2):

            @pl.loop(0, tile // wide)
            def _(k):
                cols = pl.ds(pl.multiple_of(i * tile + k * wide, wide), wide)
                back = dot_nt(ry2[here, :width], wd[cols, :])
                a = av[:, cols]
                b = bv[:, cols]
                w = jnp.tile(ry2[here, width:].astype(F32), (1, wide // LANES))
                sig = jax.nn.sigmoid(a)
                silu = a * sig
                hidden = (silu * b).astype(BF)
                piece = back * hidden.astype(F32)
                total = piece[:, :LANES]
                for n in range(1, wide // LANES):
                    total = total + piece[:, n * LANES : (n + 1) * LANES]
                score[...] += total
                grad = back * w
                d2[c, 0, :, cols] = (grad * b * sig * (1.0 + a * (1.0 - sig))).astype(BF)
                d2[c, 1, :, cols] = (grad * silu).astype(BF)

            for copy in all_d(c, i):
                copy.start()
            keep_d(c, i).start()
        ssend2[here, :] = jnp.broadcast_to(
            jnp.sum(score[...], axis=1, keepdims=True), (part, LANES)
        ).astype(BF)
        for q in range(max(1, c * size), (c + 1) * size):
            send_c(q).start()
        if c == 0:
            own_c.start()

    def send_c(q):
        z, x = source(q)
        return copy_to(
            ssend.at[slab(q)], sret.at[slab(me_e)], csend.at[q], crecv.at[q], me_d, z * n_x + x
        )

    own_c = pltpu.make_async_copy(ssend.at[slab(0)], sret.at[slab(me_e)], lsem.at[4])

    def landing(c):
        return rr.at[:, (pos_z + c) % 2, :, me_e]

    def send_r(c, q):
        return copy_to(
            rg.at[c, q],
            landing(c),
            rsend.at[c * n_ex + q],
            rrecv.at[c * n_ex + q],
            me_d,
            to(q),
        )

    def keep_r(c):
        return pltpu.make_async_copy(rg.at[c, 0], landing(c), lsem.at[5 + c])

    def row_stage(c):
        for q in list(range(1, n_ex)) + [0]:
            span = pl.ds(pl.multiple_of(to(q) * feat, 16), feat)
            grad = (dot_nt(d2[c, 0], wg[span, :]) + dot_nt(d2[c, 1], wu[span, :])).astype(BF)
            for n in range(size):
                z, x = source(c * size + n)
                rg[c, q, z // 2, x] = grad[n * cap : (n + 1) * cap, :].reshape(eights, 8, feat)
            if q:
                send_r(c, q).start()
            else:
                keep_r(c).start()

    def relay_stage(c):
        for r in hops:
            relay_p(c, r).wait_recv()
            relay_p(c, r).start()

    def transpose_stage(c):
        keep_p(c).wait()

        @pl.loop(0, n_y)
        def _(r):
            g = ((pos_y + r) % n_y) * 2 + 1 - core
            here = xg.at[c, group8(g)]
            copy_to(here, here, qsend.at[0], precv.at[c * n_dp + g], other, me_e).wait_recv()

        base = c * n_dp * part
        for m in range(deep // LANES):
            xtt[m * LANES : (m + 1) * LANES, :] = xg2[
                base : base + n_dp * part, m * LANES : (m + 1) * LANES
            ].T

    def gathered(c, i):
        keep_d(c, i).wait()
        arrived_d(c, i, other)
        for r in range(1, n_y):
            chip = (pos_y + r) % n_y

            for side in range(2):
                g = chip * 2 + side
                if far and r == 1:
                    @pl.when(core == 0)
                    def _():
                        arrived_d(c, i, g)

                elif far and r == n_y - 1:

                    @pl.when(core == 1)
                    def _():
                        arrived_d(c, i, g)

                else:
                    arrived_d(c, i, g)

    def own_half(i, out):
        cols = pl.ds(pl.multiple_of(i * wide, wide), wide)
        return pltpu.make_async_copy(wo.at[core, :, cols], out.at[:, cols], oloc.at[i])

    def other_half(i, out):
        cols = pl.ds(pl.multiple_of(i * wide, wide), wide)
        return copy_to(
            wo.at[1 - core, :, cols],
            out.at[:, cols],
            osend.at[i],
            orecv.at[i],
            other,
            me_e,
        )

    forward_stage(0)
    hidden_stage(0)
    relay_stage(0)
    row_stage(0)
    forward_stage(1)
    pass_on(0)
    hidden_stage(1)
    relay_stage(1)
    row_stage(1)

    transpose_stage(0)
    for i in range(2):
        gathered(0, i)

    @pl.loop(0, n_w)
    def _(i):
        cols = pl.ds(pl.multiple_of(i * wide, wide), wide)
        acc[:, cols] = jnp.dot(xtt[...], dg[0, :, cols], preferred_element_type=F32)

    pass_on(1)
    transpose_stage(1)

    for q in range(1, n_ex):
        send_t(q).wait_recv()
    for c in range(2):
        keep_r(c).wait()
        for q in range(1, n_ex):
            send_r(c, q).wait_recv()

    lane_no = lax.broadcasted_iota(jnp.int32, (tok, rows), 1).astype(F32)
    for s in range(n_ex):
        z, x = s // n_x, s % n_x
        column = tgt[s].T
        hit = (lane_no == column[:, 0:1]) | (lane_no == column[:, 1:2])
        choose = hit.astype(F32).astype(BF)
        place_no = ((z // 2) * 2 + z % 2) * n_x + x
        gt_ref[s * tok : (s + 1) * tok, :] = jnp.dot(
            choose, rr2[place_no], preferred_element_type=F32
        ).astype(BF)

    for i in range(2):
        gathered(1, i)

    @pl.loop(0, n_w)
    def _(i):
        cols = pl.ds(pl.multiple_of(i * wide, wide), wide)
        total = acc[:, cols] + jnp.dot(xtt[...], dg[1, :, cols], preferred_element_type=F32)
        total = (total * (1.0 / n_dp)).astype(BF)
        wo[0, :, cols] = total[:half]
        wo[1, :, cols] = total[half:]

        @pl.when(core == 0)
        def _():
            own_half(i, gg_hbm).start()
            other_half(i, gg_hbm).start()

        @pl.when(core == 1)
        def _():
            own_half(i, gu_hbm).start()
            other_half(i, gu_hbm).start()

    own_c.wait()
    for q in range(1, n_ex):
        send_c(q).wait_recv()
    column = tgt[me_e].T
    back_scores = sret2[...]
    first = jnp.dot(
        (lane_no == column[:, 0:1]).astype(F32).astype(BF), back_scores, preferred_element_type=F32
    )
    second = jnp.dot(
        (lane_no == column[:, 1:2]).astype(F32).astype(BF), back_scores, preferred_element_type=F32
    )
    which = lax.broadcasted_iota(jnp.int32, (tok, LANES), 1)
    gs_ref[...] = jnp.where(which == 0, first, second).astype(BF)[:, :2]

    for q in range(1, n_ex):
        send_t(q).wait_send()
        send_x(q).wait_send()
        send_y(q).wait_send()
        send_c(q).wait_send()
        for c in range(2):
            send_r(c, q).wait_send()
    for c in range(2):
        give_p(c).wait_send()
        for r in hops:
            send_p(c, r).wait_send()
            relay_p(c, r).wait_send()
        for i in range(2):
            for copy in all_d(c, i):
                copy.wait_send()
            if far:
                for side in range(2):
                    forward(c, i, side).wait_send()

    @pl.loop(0, n_w)
    def _(i):
        own_half(i, gg_hbm).wait()
        other_half(i, gg_hbm).wait()


def local(tokens, cotangent, gates, expert_ids, gate_w, up_w, down_w):
    tok, width = tokens.shape
    top = expert_ids.shape[1]
    n_ex = lax.axis_size("expert")
    n_dp = lax.axis_size("dp")
    cap = 3 * tok * top // (2 * n_ex)
    hid = gate_w.shape[2]
    rows = n_ex * cap
    feat = width // n_ex
    n_y = n_dp // 2
    deep = width // n_y
    n_w = hid // min(256, hid)
    vmem = pl.BlockSpec(memory_space=pltpu.VMEM)
    hbm = pl.BlockSpec(memory_space=pl.ANY)
    dma = pltpu.SemaphoreType.DMA
    part = rows // 2
    n_z, n_x = grid_of(n_ex)
    scratch = [
        pltpu.VMEM((width, hid), BF),
        pltpu.VMEM((width, hid), BF),
        pltpu.VMEM((hid, width), BF),
        pltpu.VMEM((tok, width), BF),
        pltpu.VMEM((n_ex, 8, tok), F32),
        pltpu.VMEM((rows // 8, 8, width), BF),
        pltpu.VMEM((rows // 8, 8, width + LANES), BF),
        pltpu.VMEM((rows // 8, 8, width), BF),
        pltpu.VMEM((rows // 8, 8, width + LANES), BF),
        pltpu.VMEM((part, hid), F32),
        pltpu.VMEM((part, hid), F32),
        pltpu.VMEM((2, 2, part, hid), BF),
        pltpu.VMEM((part, LANES), F32),
        pltpu.VMEM((rows // 8, 8, LANES), BF),
        pltpu.VMEM((rows // 8, 8, LANES), BF),
        pltpu.VMEM((2, n_ex, n_z // 2, n_x, cap // 8, 8, feat), BF),
        pltpu.VMEM((n_z // 2, 2, n_x, n_ex, cap // 8, 8, feat), BF),
        pltpu.VMEM((2, n_dp * part // 8, 8, deep), BF),
        pltpu.VMEM((2, n_dp * part, hid), BF),
        pltpu.VMEM((deep, n_dp * part), BF),
        pltpu.VMEM((deep, hid), F32),
        pltpu.VMEM((2, deep // 2, hid), BF),
        dma((3,)),
        dma((n_ex,)),
        dma((n_ex,)),
        dma((n_ex,)),
        dma((n_ex,)),
        dma((n_ex,)),
        dma((n_ex,)),
        dma((2 * n_y,)),
        dma((2 * n_dp,)),
        dma((2 * n_y,)),
        dma((8 * n_y,)),
        dma((4 * n_dp,)),
        dma((8,)),
        dma((4,)),
        dma((2 * n_ex,)),
        dma((2 * n_ex,)),
        dma((n_ex,)),
        dma((n_ex,)),
        dma((n_w,)),
        dma((n_w,)),
        dma((n_w,)),
        dma((9,)),
    ]
    return pl.pallas_call(
        functools.partial(kernel, n_dp, n_ex, cap),
        out_shape=(
            jax.ShapeDtypeStruct((n_ex * tok, feat), BF),
            jax.ShapeDtypeStruct((width // n_dp, hid), BF),
            jax.ShapeDtypeStruct((width // n_dp, hid), BF),
            jax.ShapeDtypeStruct((tok, top), BF),
        ),
        in_specs=[vmem, vmem, hbm, hbm, hbm, hbm, hbm],
        out_specs=(vmem, hbm, hbm, vmem),
        scratch_shapes=scratch,
        compiler_params=pltpu.CompilerParams(
            collective_id=0, has_side_effects=True, vmem_limit_bytes=64 * 1024 * 1024
        ),
    )(
        expert_ids.T,
        gates.T,
        tokens,
        cotangent,
        gate_w[0],
        up_w[0],
        down_w[0],
    )


def settle(*refs):
    count = (len(refs) - 1) // 2
    copies = [
        pltpu.make_async_copy(refs[k], refs[count + k], refs[-1].at[k]) for k in range(count)
    ]
    for copy in copies:
        copy.start()
    for copy in copies:
        copy.wait()


def shard(tokens, cotangent, gates, expert_ids, gate_w, up_w, down_w):
    results = local(tokens, cotangent, gates, expert_ids, gate_w, up_w, down_w)
    hbm = pl.BlockSpec(memory_space=pl.ANY)
    grad_tokens, grad_gate, grad_up, grad_gates = pl.pallas_call(
        settle,
        out_shape=tuple(jax.ShapeDtypeStruct(r.shape, r.dtype) for r in results),
        in_specs=[hbm] * 4,
        out_specs=(hbm,) * 4,
        scratch_shapes=[pltpu.SemaphoreType.DMA((4,))],
    )(*results)
    return grad_tokens, grad_gate[None], grad_up[None], grad_gates


def solution(mesh):
    placed = (
        P(("dp", "expert"), None),
        P(("dp", "expert"), None),
        P(("dp", "expert"), None),
        P(("dp", "expert"), None),
        P("expert", None, None),
        P("expert", None, None),
        P("expert", None, None),
    )
    return jax.shard_map(
        shard,
        mesh=mesh,
        in_specs=placed,
        out_specs=(
            P("dp", "expert"),
            P("expert", "dp", None),
            P("expert", "dp", None),
            P(("dp", "expert"), None),
        ),
        check_vma=False,
    )
```

```python
import functools
import jax
import jax.numpy as jnp
from jax import lax
from jax.experimental import pallas as pl
from jax.experimental.pallas import tpu as pltpu
from jax.sharding import PartitionSpec as P

MESH = pl.DeviceIdType.MESH
BF = jnp.bfloat16
F32 = jnp.float32
LANES = 128


def grid_of(count):
    side = 1
    while side * side * 4 <= count:
        side *= 2
    return count // side, side


def dot_nt(left, right):
    return lax.dot_general(left, right, (((1,), (1,)), ((), ())), preferred_element_type=F32)


def kernel(
    n_dp,
    n_ex,
    cap,
    ids_ref,
    gts_ref,
    x_hbm,
    y_hbm,
    wg_hbm,
    wu_hbm,
    wd_hbm,
    gt_ref,
    gg_hbm,
    gu_hbm,
    gs_ref,
    wg,
    wu,
    wd,
    held,
    tgt,
    sx,
    sy,
    rx,
    ry,
    av,
    bv,
    d2,
    score,
    wrow,
    ssend,
    sret,
    rg,
    rr,
    xg,
    dg,
    xtt,
    acc,
    wo,
    wsem,
    tsend,
    trecv,
    xsend,
    xrecv,
    ysend,
    yrecv,
    psend,
    precv,
    qsend,
    dsend,
    drecv,
    fsend,
    dloc,
    rsend,
    rrecv,
    csend,
    crecv,
    osend,
    orecv,
    oloc,
    lsem,
):
    n_z, n_x = grid_of(n_ex)
    n_y = n_dp // 2
    tok, width = held.shape
    hid = wg.shape[1]
    rows = n_ex * cap
    part = rows // 2
    eights = cap // 8
    span8 = part // 8
    feat = width // n_ex
    deep = width // n_y
    half = deep // 2
    tile = hid // 2
    wide = min(256, hid)
    n_w = hid // wide
    me_e = lax.axis_index("expert")
    me_d = lax.axis_index("dp")
    pos_z, pos_x = me_e // n_x, me_e % n_x
    pos_y, core = me_d // 2, me_d % 2
    other = me_d + 1 - 2 * core
    near = sorted({1, n_y - 1})
    hops = [r for r in [n_y // 2] + near if r]
    hops = sorted(set(hops), key=hops.index)

    signs = [(a, b) for b in range(n_x) for a in range(n_z)]
    signs.sort(key=lambda t: (min(t[0], n_z - t[0]) + min(t[1], n_x - t[1]), t))
    order = [t for t in signs if t[0] % 2 == 0] + [t for t in signs if t[0] % 2 == 1]
    size = n_ex // 2

    def to(q):
        return ((pos_z + order[q][0]) % n_z) * n_x + (pos_x + order[q][1]) % n_x

    def source(q):
        return ((pos_z + n_z - order[q][0]) % n_z), (pos_x + n_x - order[q][1]) % n_x

    def copy_to(src, dst, send, recv, dp_id, ex_id):
        return pltpu.make_async_remote_copy(
            src_ref=src,
            dst_ref=dst,
            send_sem=send,
            recv_sem=recv,
            device_id=(dp_id, ex_id),
            device_id_type=MESH,
        )

    def slab(o):
        return pl.ds(o * eights, eights)

    def tiles(i):
        return slice(i * tile, (i + 1) * tile)

    sx2, rx2 = sx.reshape(rows, width), rx.reshape(rows, width)
    sy2, ry2 = sy.reshape(rows, width), ry.reshape(rows, width)
    ssend2, sret2 = ssend.reshape(rows, LANES), sret.reshape(rows, LANES)
    xg2 = xg.reshape(2 * n_dp * part, deep)
    rr2 = rr.reshape(n_ex, rows, feat)

    load_x = pltpu.make_async_copy(x_hbm, held, lsem.at[7])
    load_y = pltpu.make_async_copy(y_hbm, held, lsem.at[8])
    load_x.start()
    loads = [
        pltpu.make_async_copy(wg_hbm, wg, wsem.at[0]),
        pltpu.make_async_copy(wu_hbm, wu, wsem.at[1]),
        pltpu.make_async_copy(wd_hbm, wd, wsem.at[2]),
    ]
    for load in loads:
        load.start()

    barrier = pltpu.get_barrier_semaphore()

    @pl.loop(1, n_ex)
    def _(o):
        partner = ((pos_z + o // n_x) % n_z) * n_x + (pos_x + o % n_x) % n_x
        pl.semaphore_signal(barrier, inc=1, device_id=(me_d, partner), device_id_type=MESH)

    @pl.loop(1, n_dp)
    def _(o):
        pl.semaphore_signal(
            barrier, inc=1, device_id=((me_d + o) % n_dp, me_e), device_id_type=MESH
        )

    ids = ids_ref[...]
    expert_no = lax.broadcasted_iota(jnp.int32, (n_ex, tok), 0)
    named = [(expert_no == ids[k : k + 1, :]).astype(F32) for k in range(2)]
    before = (
        lax.broadcasted_iota(jnp.int32, (tok, tok), 0)
        < lax.broadcasted_iota(jnp.int32, (tok, tok), 1)
    ).astype(F32)
    count = jnp.dot(
        (named[0] + named[1]).astype(BF), before.astype(BF), preferred_element_type=F32
    )
    place = [
        jnp.sum(named[k] * count, axis=0, keepdims=True) + (ids[k : k + 1, :] * cap).astype(F32)
        for k in range(2)
    ]
    slot_no = lax.broadcasted_iota(jnp.int32, (rows, tok), 0).astype(F32)
    picks = [(slot_no == place[k]).astype(F32) for k in range(2)]
    pick = (picks[0] + picks[1]).astype(BF)
    gts = gts_ref[...].astype(F32)
    tgt[me_e, 0:2, :] = jnp.concatenate(place, axis=0)
    tgt[me_e, 2:4, :] = gts
    tgt[me_e, 4:8, :] = jnp.zeros((4, tok), F32)

    def send_x(q):
        e = to(q)
        return copy_to(sx.at[slab(e)], rx.at[slab(q)], xsend.at[q], xrecv.at[q], me_d, e)

    def send_y(q):
        e = to(q)
        return copy_to(sy.at[slab(e)], ry.at[slab(q)], ysend.at[q], yrecv.at[q], me_d, e)

    def leave(src, dst, send, recv, chosen):
        for n in range(eights):
            for q in chosen:
                e = to(q)
                copy_to(
                    src.at[e * eights + n], dst.at[q * eights + n], send.at[q], recv.at[q], me_d, e
                ).start()

    def send_t(q):
        return copy_to(tgt.at[me_e], tgt.at[me_e], tsend.at[q], trecv.at[q], me_d, to(q))

    block = min(512, width)
    load_x.wait()
    for i in range(width // block):
        span = slice(i * block, (i + 1) * block)
        sx2[:, span] = jnp.dot(pick, held[:, span], preferred_element_type=F32).astype(BF)

    load_y.start()
    pl.semaphore_wait(barrier, n_ex - 1 + n_dp - 1)
    for q in range(1, n_ex):
        send_t(q).start()
    leave(sx, rx, xsend, xrecv, range(1, size))
    own_x = pltpu.make_async_copy(sx.at[slab(me_e)], rx.at[slab(0)], lsem.at[0])
    own_x.start()
    load_y.wait()
    for i in range(width // block):
        span = slice(i * block, (i + 1) * block)
        sy2[:, span] = jnp.dot(pick, held[:, span], preferred_element_type=F32).astype(BF)
    leave(sy, ry, ysend, yrecv, range(1, size))
    own_y = pltpu.make_async_copy(sy.at[slab(me_e)], ry.at[slab(0)], lsem.at[1])
    own_y.start()
    leave(sx, rx, xsend, xrecv, range(size, n_ex))
    leave(sy, ry, ysend, yrecv, range(size, n_ex))

    def features(chip):
        return pl.ds(pl.multiple_of(chip * deep, LANES), deep)

    def group8(g):
        return pl.ds(g * span8, span8)

    def send_p(c, r):
        chip = (pos_y + r) % n_y
        return copy_to(
            rx.at[c * span8 : (c + 1) * span8, :, features(chip)],
            xg.at[c, group8(me_d)],
            psend.at[c * n_y + r],
            precv.at[c * n_dp + me_d],
            chip * 2 + core,
            me_e,
        )

    def keep_p(c):
        return pltpu.make_async_copy(
            rx.at[c * span8 : (c + 1) * span8, :, features(pos_y)],
            xg.at[c, group8(me_d)],
            lsem.at[2 + c],
        )

    def give_p(c):
        return copy_to(
            rx.at[c * span8 : (c + 1) * span8, :, features(pos_y)],
            xg.at[c, group8(me_d)],
            qsend.at[c * n_y],
            precv.at[c * n_dp + me_d],
            other,
            me_e,
        )

    def relay_p(c, r):
        g = ((pos_y + n_y - r) % n_y) * 2 + core
        return copy_to(
            xg.at[c, group8(g)],
            xg.at[c, group8(g)],
            qsend.at[c * n_y + r],
            precv.at[c * n_dp + g],
            other,
            me_e,
        )

    def group(g):
        return pl.ds(pl.multiple_of(g * part, 16), part)

    def send_d(c, i, r, which):
        side = core if which == 0 else 1 - core
        chip = (pos_y + r) % n_y
        return copy_to(
            d2.at[c, side, :, tiles(i)],
            dg.at[c, group(me_d), tiles(i)],
            dsend.at[((c * 2 + i) * n_y + r) * 2 + which],
            drecv.at[(c * 2 + i) * n_dp + me_d],
            chip * 2 + side,
            me_e,
        )

    def keep_d(c, i):
        return pltpu.make_async_copy(
            d2.at[c, core, :, tiles(i)], dg.at[c, group(me_d), tiles(i)], dloc.at[c * 2 + i]
        )

    def all_d(c, i):
        return [send_d(c, i, r, which) for r in near for which in (0, 1)] + [send_d(c, i, 0, 1)]

    def forward(c, i, side):
        origin = (pos_y + n_y - 1 + 2 * core) % n_y
        g = origin * 2 + side
        return copy_to(
            dg.at[c, group(g), tiles(i)],
            dg.at[c, group(g), tiles(i)],
            fsend.at[(c * 2 + i) * 2 + side],
            drecv.at[(c * 2 + i) * n_dp + g],
            ((pos_y + n_y + 1 - 2 * core) % n_y) * 2 + core,
            me_e,
        )

    def arrived_d(c, i, g):
        here = dg.at[c, group(g), tiles(i)]
        copy_to(here, here, fsend.at[0], drecv.at[(c * 2 + i) * n_dp + g], other, me_e).wait_recv()

    far = n_y > 2

    def pass_on(c):
        if far:
            for i in range(2):
                for side in range(2):
                    forward(c, i, side).wait_recv()
                    forward(c, i, side).start()

    def forward_stage(c):
        if c == 0:
            own_x.wait()
        for q in range(max(1, c * size), (c + 1) * size):
            send_x(q).wait_recv()
        for r in hops:
            send_p(c, r).start()
        keep_p(c).start()
        give_p(c).start()
        if c == 0:
            loads[0].wait()
            loads[1].wait()
        here = slice(c * part, (c + 1) * part)

        @pl.loop(0, n_w)
        def _(i):
            cols = pl.ds(pl.multiple_of(i * wide, wide), wide)
            av[:, cols] = jnp.dot(rx2[here, :], wg[:, cols], preferred_element_type=F32)
            bv[:, cols] = jnp.dot(rx2[here, :], wu[:, cols], preferred_element_type=F32)

    def hidden_stage(c):
        if c == 0:
            own_y.wait()
            loads[2].wait()
        for q in range(max(1, c * size), (c + 1) * size):
            send_y(q).wait_recv()
        here = slice(c * part, (c + 1) * part)
        if c == 0:
            for q in range(1, n_ex):
                send_t(q).wait_recv()
            slot_here = lax.broadcasted_iota(jnp.int32, (cap, tok), 0).astype(F32)
            slot_here = slot_here + (me_e * cap).astype(F32)
            for q in range(n_ex):
                z, x = source(q)
                note = tgt[z * n_x + x]
                fit = jnp.where(slot_here == note[0:1, :], note[2:3, :], 0.0)
                fit = fit + jnp.where(slot_here == note[1:2, :], note[3:4, :], 0.0)
                fit = jnp.sum(fit, axis=1, keepdims=True)
                wrow[q * cap : (q + 1) * cap, :] = jnp.broadcast_to(fit, (cap, LANES))
        score[...] = jnp.zeros_like(score)
        for i in range(2):

            @pl.loop(0, tile // wide)
            def _(k):
                cols = pl.ds(pl.multiple_of(i * tile + k * wide, wide), wide)
                back = dot_nt(ry2[here, :], wd[cols, :])
                a = av[:, cols]
                b = bv[:, cols]
                w = jnp.tile(wrow[here, :], (1, wide // LANES))
                sig = jax.nn.sigmoid(a)
                silu = a * sig
                hidden = (silu * b).astype(BF)
                piece = back * hidden.astype(F32)
                total = piece[:, :LANES]
                for n in range(1, wide // LANES):
                    total = total + piece[:, n * LANES : (n + 1) * LANES]
                score[...] += total
                grad = back * w
                d2[c, 0, :, cols] = (grad * b * sig * (1.0 + a * (1.0 - sig))).astype(BF)
                d2[c, 1, :, cols] = (grad * silu).astype(BF)

            for copy in all_d(c, i):
                copy.start()
            keep_d(c, i).start()
        ssend2[here, :] = jnp.broadcast_to(
            jnp.sum(score[...], axis=1, keepdims=True), (part, LANES)
        ).astype(BF)
        for q in range(max(1, c * size), (c + 1) * size):
            send_c(q).start()
        if c == 0:
            own_c.start()

    def send_c(q):
        z, x = source(q)
        return copy_to(
            ssend.at[slab(q)], sret.at[slab(me_e)], csend.at[q], crecv.at[q], me_d, z * n_x + x
        )

    own_c = pltpu.make_async_copy(ssend.at[slab(0)], sret.at[slab(me_e)], lsem.at[4])

    def landing(c):
        return rr.at[:, (pos_z + c) % 2, :, me_e]

    def send_r(c, q):
        return copy_to(
            rg.at[c, q],
            landing(c),
            rsend.at[c * n_ex + q],
            rrecv.at[c * n_ex + q],
            me_d,
            to(q),
        )

    def keep_r(c):
        return pltpu.make_async_copy(rg.at[c, 0], landing(c), lsem.at[5 + c])

    def row_stage(c):
        for q in list(range(1, n_ex)) + [0]:
            span = pl.ds(pl.multiple_of(to(q) * feat, 16), feat)
            grad = (dot_nt(d2[c, 0], wg[span, :]) + dot_nt(d2[c, 1], wu[span, :])).astype(BF)
            for n in range(size):
                z, x = source(c * size + n)
                rg[c, q, z // 2, x] = grad[n * cap : (n + 1) * cap, :].reshape(eights, 8, feat)
            if q:
                send_r(c, q).start()
            else:
                keep_r(c).start()

    def relay_stage(c):
        for r in hops:
            relay_p(c, r).wait_recv()
            relay_p(c, r).start()

    def transpose_stage(c):
        keep_p(c).wait()

        @pl.loop(0, n_y)
        def _(r):
            g = ((pos_y + r) % n_y) * 2 + 1 - core
            here = xg.at[c, group8(g)]
            copy_to(here, here, qsend.at[0], precv.at[c * n_dp + g], other, me_e).wait_recv()

        base = c * n_dp * part
        for m in range(deep // LANES):
            xtt[m * LANES : (m + 1) * LANES, :] = xg2[
                base : base + n_dp * part, m * LANES : (m + 1) * LANES
            ].T

    def gathered(c, i):
        keep_d(c, i).wait()
        arrived_d(c, i, other)
        for r in range(1, n_y):
            chip = (pos_y + r) % n_y

            for side in range(2):
                g = chip * 2 + side
                if far and r == 1:
                    @pl.when(core == 0)
                    def _():
                        arrived_d(c, i, g)

                elif far and r == n_y - 1:

                    @pl.when(core == 1)
                    def _():
                        arrived_d(c, i, g)

                else:
                    arrived_d(c, i, g)

    def own_half(i, out):
        cols = pl.ds(pl.multiple_of(i * wide, wide), wide)
        return pltpu.make_async_copy(wo.at[core, :, cols], out.at[:, cols], oloc.at[i])

    def other_half(i, out):
        cols = pl.ds(pl.multiple_of(i * wide, wide), wide)
        return copy_to(
            wo.at[1 - core, :, cols],
            out.at[:, cols],
            osend.at[i],
            orecv.at[i],
            other,
            me_e,
        )

    forward_stage(0)
    hidden_stage(0)
    relay_stage(0)
    row_stage(0)
    forward_stage(1)
    pass_on(0)
    hidden_stage(1)
    relay_stage(1)
    row_stage(1)

    transpose_stage(0)
    for i in range(2):
        gathered(0, i)

    @pl.loop(0, n_w)
    def _(i):
        cols = pl.ds(pl.multiple_of(i * wide, wide), wide)
        acc[:, cols] = jnp.dot(xtt[...], dg[0, :, cols], preferred_element_type=F32)

    pass_on(1)
    transpose_stage(1)

    for c in range(2):
        keep_r(c).wait()
        for q in range(1, n_ex):
            send_r(c, q).wait_recv()

    for s in range(n_ex):
        z, x = s // n_x, s % n_x
        note = tgt[s]
        choose = ((slot_no == note[0:1, :]) | (slot_no == note[1:2, :])).astype(F32).astype(BF)
        place_no = ((z // 2) * 2 + z % 2) * n_x + x
        gt_ref[:, s * tok : (s + 1) * tok] = lax.dot_general(
            rr2[place_no], choose, (((0,), (0,)), ((), ())), preferred_element_type=F32
        ).astype(BF)

    for i in range(2):
        gathered(1, i)

    @pl.loop(0, n_w)
    def _(i):
        cols = pl.ds(pl.multiple_of(i * wide, wide), wide)
        total = acc[:, cols] + jnp.dot(xtt[...], dg[1, :, cols], preferred_element_type=F32)
        total = (total * (1.0 / n_dp)).astype(BF)
        wo[0, :, cols] = total[:half]
        wo[1, :, cols] = total[half:]

        @pl.when(core == 0)
        def _():
            own_half(i, gg_hbm).start()
            other_half(i, gg_hbm).start()

        @pl.when(core == 1)
        def _():
            own_half(i, gu_hbm).start()
            other_half(i, gu_hbm).start()

    own_c.wait()
    for q in range(1, n_ex):
        send_c(q).wait_recv()
    back_scores = sret2[...].astype(F32)
    note = tgt[me_e]
    for k in range(2):
        found = jnp.where(slot_no == note[k : k + 1, :], back_scores, 0.0)
        gs_ref[k : k + 1, :] = jnp.sum(found, axis=0, keepdims=True).astype(BF)

    for q in range(1, n_ex):
        send_t(q).wait_send()
        send_x(q).wait_send()
        send_y(q).wait_send()
        send_c(q).wait_send()
        for c in range(2):
            send_r(c, q).wait_send()
    for c in range(2):
        give_p(c).wait_send()
        for r in hops:
            send_p(c, r).wait_send()
            relay_p(c, r).wait_send()
        for i in range(2):
            for copy in all_d(c, i):
                copy.wait_send()
            if far:
                for side in range(2):
                    forward(c, i, side).wait_send()

    @pl.loop(0, n_w)
    def _(i):
        own_half(i, gg_hbm).wait()
        other_half(i, gg_hbm).wait()


def local(tokens, cotangent, gates, expert_ids, gate_w, up_w, down_w):
    tok, width = tokens.shape
    top = expert_ids.shape[1]
    n_ex = lax.axis_size("expert")
    n_dp = lax.axis_size("dp")
    cap = 3 * tok * top // (2 * n_ex)
    hid = gate_w.shape[2]
    rows = n_ex * cap
    feat = width // n_ex
    n_y = n_dp // 2
    deep = width // n_y
    n_w = hid // min(256, hid)
    vmem = pl.BlockSpec(memory_space=pltpu.VMEM)
    hbm = pl.BlockSpec(memory_space=pl.ANY)
    dma = pltpu.SemaphoreType.DMA
    part = rows // 2
    n_z, n_x = grid_of(n_ex)
    scratch = [
        pltpu.VMEM((width, hid), BF),
        pltpu.VMEM((width, hid), BF),
        pltpu.VMEM((hid, width), BF),
        pltpu.VMEM((tok, width), BF),
        pltpu.VMEM((n_ex, 8, tok), F32),
        pltpu.VMEM((rows // 8, 8, width), BF),
        pltpu.VMEM((rows // 8, 8, width), BF),
        pltpu.VMEM((rows // 8, 8, width), BF),
        pltpu.VMEM((rows // 8, 8, width), BF),
        pltpu.VMEM((part, hid), F32),
        pltpu.VMEM((part, hid), F32),
        pltpu.VMEM((2, 2, part, hid), BF),
        pltpu.VMEM((part, LANES), F32),
        pltpu.VMEM((rows, LANES), F32),
        pltpu.VMEM((rows // 8, 8, LANES), BF),
        pltpu.VMEM((rows // 8, 8, LANES), BF),
        pltpu.VMEM((2, n_ex, n_z // 2, n_x, cap // 8, 8, feat), BF),
        pltpu.VMEM((n_z // 2, 2, n_x, n_ex, cap // 8, 8, feat), BF),
        pltpu.VMEM((2, n_dp * part // 8, 8, deep), BF),
        pltpu.VMEM((2, n_dp * part, hid), BF),
        pltpu.VMEM((deep, n_dp * part), BF),
        pltpu.VMEM((deep, hid), F32),
        pltpu.VMEM((2, deep // 2, hid), BF),
        dma((3,)),
        dma((n_ex,)),
        dma((n_ex,)),
        dma((n_ex,)),
        dma((n_ex,)),
        dma((n_ex,)),
        dma((n_ex,)),
        dma((2 * n_y,)),
        dma((2 * n_dp,)),
        dma((2 * n_y,)),
        dma((8 * n_y,)),
        dma((4 * n_dp,)),
        dma((8,)),
        dma((4,)),
        dma((2 * n_ex,)),
        dma((2 * n_ex,)),
        dma((n_ex,)),
        dma((n_ex,)),
        dma((n_w,)),
        dma((n_w,)),
        dma((n_w,)),
        dma((9,)),
    ]
    return pl.pallas_call(
        functools.partial(kernel, n_dp, n_ex, cap),
        out_shape=(
            jax.ShapeDtypeStruct((feat, n_ex * tok), BF),
            jax.ShapeDtypeStruct((width // n_dp, hid), BF),
            jax.ShapeDtypeStruct((width // n_dp, hid), BF),
            jax.ShapeDtypeStruct((top, tok), BF),
        ),
        in_specs=[vmem, vmem, hbm, hbm, hbm, hbm, hbm],
        out_specs=(vmem, hbm, hbm, vmem),
        scratch_shapes=scratch,
        compiler_params=pltpu.CompilerParams(
            collective_id=0, has_side_effects=True, vmem_limit_bytes=64 * 1024 * 1024
        ),
    )(
        expert_ids.T,
        gates.T,
        tokens,
        cotangent,
        gate_w[0],
        up_w[0],
        down_w[0],
    )


def settle(*refs):
    for k in range(4):
        refs[4 + k][...] = refs[k][...]


def shard(tokens, cotangent, gates, expert_ids, gate_w, up_w, down_w):
    results = local(tokens, cotangent, gates, expert_ids, gate_w, up_w, down_w)
    steps = 7
    specs = [pl.BlockSpec((r.shape[0] // steps, r.shape[1]), lambda i: (i, 0)) for r in results[:3]]
    specs.append(pl.BlockSpec(results[3].shape, lambda i: (0, 0)))
    grad_tokens, grad_gate, grad_up, grad_gates = pl.pallas_call(
        settle,
        out_shape=tuple(jax.ShapeDtypeStruct(r.shape, r.dtype) for r in results),
        grid=(steps,),
        in_specs=specs,
        out_specs=tuple(specs),
    )(*results)
    return grad_tokens.T, grad_gate[None], grad_up[None], grad_gates.T


def solution(mesh):
    placed = (
        P(("dp", "expert"), None),
        P(("dp", "expert"), None),
        P(("dp", "expert"), None),
        P(("dp", "expert"), None),
        P("expert", None, None),
        P("expert", None, None),
        P("expert", None, None),
    )
    return jax.shard_map(
        shard,
        mesh=mesh,
        in_specs=placed,
        out_specs=(
            P("dp", "expert"),
            P("expert", "dp", None),
            P("expert", "dp", None),
            P(("dp", "expert"), None),
        ),
        check_vma=False,
    )
```

```python
import functools
import jax
import jax.numpy as jnp
from jax import lax
from jax.experimental import pallas as pl
from jax.experimental.pallas import tpu as pltpu
from jax.sharding import PartitionSpec as P

MESH = pl.DeviceIdType.MESH
BF = jnp.bfloat16
F32 = jnp.float32
LANES = 128
CHUNKS = 4


def grid_of(count):
    side = 1
    while side * side * 4 <= count:
        side *= 2
    return count // side, side


def dot_nt(left, right):
    return lax.dot_general(left, right, (((1,), (1,)), ((), ())), preferred_element_type=F32)


def kernel(
    n_dp,
    n_ex,
    cap,
    ids_ref,
    gts_ref,
    x_hbm,
    y_hbm,
    wg_hbm,
    wu_hbm,
    wd_hbm,
    gt_ref,
    gg_hbm,
    gu_hbm,
    gs_ref,
    wg,
    wu,
    wd,
    held,
    tgt,
    sx,
    sy,
    rx,
    ry,
    av,
    bv,
    d2,
    score,
    wrow,
    ssend,
    sret,
    rg,
    rr,
    xg,
    dg,
    xtt,
    acc,
    wo,
    wsem,
    tsend,
    trecv,
    xsend,
    xrecv,
    ysend,
    yrecv,
    psend,
    precv,
    qsend,
    dsend,
    drecv,
    fsend,
    dloc,
    rsend,
    rrecv,
    csend,
    crecv,
    osend,
    orecv,
    oloc,
    lsem,
):
    n_z, n_x = grid_of(n_ex)
    n_y = n_dp // 2
    tok, width = held.shape
    hid = wg.shape[1]
    rows = n_ex * cap
    part = rows // CHUNKS
    eights = cap // 8
    span8 = part // 8
    feat = width // n_ex
    deep = width // n_y
    half = deep // 2
    wide = min(256, hid)
    n_w = hid // wide
    me_e = lax.axis_index("expert")
    me_d = lax.axis_index("dp")
    pos_z, pos_x = me_e // n_x, me_e % n_x
    pos_y, core = me_d // 2, me_d % 2
    other = me_d + 1 - 2 * core
    near = sorted({1, n_y - 1})
    hops = [r for r in [n_y // 2] + near if r]
    hops = sorted(set(hops), key=hops.index)

    signs = [(a, b) for b in range(n_x) for a in range(n_z)]
    signs.sort(key=lambda t: (min(t[0], n_z - t[0]) + min(t[1], n_x - t[1]), t))
    order = [t for n in range(CHUNKS) for t in signs if (t[0] % 2) * 2 + t[1] % 2 == n]
    size = n_ex // CHUNKS

    def to(q):
        return ((pos_z + order[q][0]) % n_z) * n_x + (pos_x + order[q][1]) % n_x

    def source(q):
        return ((pos_z + n_z - order[q][0]) % n_z), (pos_x + n_x - order[q][1]) % n_x

    def copy_to(src, dst, send, recv, dp_id, ex_id):
        return pltpu.make_async_remote_copy(
            src_ref=src,
            dst_ref=dst,
            send_sem=send,
            recv_sem=recv,
            device_id=(dp_id, ex_id),
            device_id_type=MESH,
        )

    def slab(o):
        return pl.ds(o * eights, eights)

    sx2, rx2 = sx.reshape(rows, width), rx.reshape(rows, width)
    sy2, ry2 = sy.reshape(rows, width), ry.reshape(rows, width)
    ssend2, sret2 = ssend.reshape(rows, LANES), sret.reshape(rows, LANES)
    xg2 = xg.reshape(CHUNKS * n_dp * part, deep)
    rr2 = rr.reshape(n_ex, rows, feat)

    load_x = pltpu.make_async_copy(x_hbm, held, lsem.at[2])
    load_y = pltpu.make_async_copy(y_hbm, held, lsem.at[3])
    load_x.start()
    loads = [
        pltpu.make_async_copy(wg_hbm, wg, wsem.at[0]),
        pltpu.make_async_copy(wu_hbm, wu, wsem.at[1]),
        pltpu.make_async_copy(wd_hbm, wd, wsem.at[2]),
    ]
    for load in loads:
        load.start()

    barrier = pltpu.get_barrier_semaphore()

    @pl.loop(1, n_ex)
    def _(o):
        partner = ((pos_z + o // n_x) % n_z) * n_x + (pos_x + o % n_x) % n_x
        pl.semaphore_signal(barrier, inc=1, device_id=(me_d, partner), device_id_type=MESH)

    @pl.loop(1, n_dp)
    def _(o):
        pl.semaphore_signal(
            barrier, inc=1, device_id=((me_d + o) % n_dp, me_e), device_id_type=MESH
        )

    ids = ids_ref[...]
    expert_no = lax.broadcasted_iota(jnp.int32, (n_ex, tok), 0)
    named = [(expert_no == ids[k : k + 1, :]).astype(F32) for k in range(2)]
    before = (
        lax.broadcasted_iota(jnp.int32, (tok, tok), 0)
        < lax.broadcasted_iota(jnp.int32, (tok, tok), 1)
    ).astype(F32)
    count = jnp.dot(
        (named[0] + named[1]).astype(BF), before.astype(BF), preferred_element_type=F32
    )
    place = [
        jnp.sum(named[k] * count, axis=0, keepdims=True) + (ids[k : k + 1, :] * cap).astype(F32)
        for k in range(2)
    ]
    slot_no = lax.broadcasted_iota(jnp.int32, (rows, tok), 0).astype(F32)
    picks = [(slot_no == place[k]).astype(F32) for k in range(2)]
    pick = (picks[0] + picks[1]).astype(BF)
    gts = gts_ref[...].astype(F32)
    tgt[me_e, 0:2, :] = jnp.concatenate(place, axis=0)
    tgt[me_e, 2:4, :] = gts
    tgt[me_e, 4:8, :] = jnp.zeros((4, tok), F32)

    def send_x(q):
        e = to(q)
        return copy_to(sx.at[slab(e)], rx.at[slab(q)], xsend.at[q], xrecv.at[q], me_d, e)

    def send_y(q):
        e = to(q)
        return copy_to(sy.at[slab(e)], ry.at[slab(q)], ysend.at[q], yrecv.at[q], me_d, e)

    def leave(src, dst, send, recv, chosen):
        for n in range(eights):
            for q in chosen:
                e = to(q)
                copy_to(
                    src.at[e * eights + n], dst.at[q * eights + n], send.at[q], recv.at[q], me_d, e
                ).start()

    def send_t(q):
        return copy_to(tgt.at[me_e], tgt.at[me_e], tsend.at[q], trecv.at[q], me_d, to(q))

    block = min(512, width)
    load_x.wait()
    for i in range(width // block):
        span = slice(i * block, (i + 1) * block)
        sx2[:, span] = jnp.dot(pick, held[:, span], preferred_element_type=F32).astype(BF)

    load_y.start()
    pl.semaphore_wait(barrier, n_ex - 1 + n_dp - 1)
    for q in range(1, n_ex):
        send_t(q).start()
    leave(sx, rx, xsend, xrecv, range(1, size))
    own_x = pltpu.make_async_copy(sx.at[slab(me_e)], rx.at[slab(0)], lsem.at[0])
    own_x.start()
    load_y.wait()
    for i in range(width // block):
        span = slice(i * block, (i + 1) * block)
        sy2[:, span] = jnp.dot(pick, held[:, span], preferred_element_type=F32).astype(BF)
    leave(sy, ry, ysend, yrecv, range(1, size))
    own_y = pltpu.make_async_copy(sy.at[slab(me_e)], ry.at[slab(0)], lsem.at[1])
    own_y.start()
    for c in range(1, CHUNKS):
        leave(sx, rx, xsend, xrecv, range(c * size, (c + 1) * size))
        leave(sy, ry, ysend, yrecv, range(c * size, (c + 1) * size))

    def features(chip):
        return pl.ds(pl.multiple_of(chip * deep, LANES), deep)

    def group8(g):
        return pl.ds(g * span8, span8)

    def send_p(c, r):
        chip = (pos_y + r) % n_y
        return copy_to(
            rx.at[c * span8 : (c + 1) * span8, :, features(chip)],
            xg.at[c, group8(me_d)],
            psend.at[c * n_y + r],
            precv.at[c * n_dp + me_d],
            chip * 2 + core,
            me_e,
        )

    def keep_p(c):
        return pltpu.make_async_copy(
            rx.at[c * span8 : (c + 1) * span8, :, features(pos_y)],
            xg.at[c, group8(me_d)],
            lsem.at[5 + c],
        )

    def give_p(c):
        return copy_to(
            rx.at[c * span8 : (c + 1) * span8, :, features(pos_y)],
            xg.at[c, group8(me_d)],
            qsend.at[c * n_y],
            precv.at[c * n_dp + me_d],
            other,
            me_e,
        )

    def relay_p(c, r):
        g = ((pos_y + n_y - r) % n_y) * 2 + core
        return copy_to(
            xg.at[c, group8(g)],
            xg.at[c, group8(g)],
            qsend.at[c * n_y + r],
            precv.at[c * n_dp + g],
            other,
            me_e,
        )

    def group(g):
        return pl.ds(pl.multiple_of(g * part, 16), part)

    def send_d(c, r, which):
        side = core if which == 0 else 1 - core
        chip = (pos_y + r) % n_y
        return copy_to(
            d2.at[c, side],
            dg.at[c, group(me_d)],
            dsend.at[(c * n_y + r) * 2 + which],
            drecv.at[c * n_dp + me_d],
            chip * 2 + side,
            me_e,
        )

    def keep_d(c):
        return pltpu.make_async_copy(d2.at[c, core], dg.at[c, group(me_d)], dloc.at[c])

    def all_d(c):
        return [send_d(c, r, which) for r in near for which in (0, 1)] + [send_d(c, 0, 1)]

    def forward(c, side):
        origin = (pos_y + n_y - 1 + 2 * core) % n_y
        g = origin * 2 + side
        return copy_to(
            dg.at[c, group(g)],
            dg.at[c, group(g)],
            fsend.at[c * 2 + side],
            drecv.at[c * n_dp + g],
            ((pos_y + n_y + 1 - 2 * core) % n_y) * 2 + core,
            me_e,
        )

    def arrived_d(c, g):
        here = dg.at[c, group(g)]
        copy_to(here, here, fsend.at[0], drecv.at[c * n_dp + g], other, me_e).wait_recv()

    far = n_y > 2

    def pass_on(c):
        if far:
            for side in range(2):
                forward(c, side).wait_recv()
                forward(c, side).start()

    def forward_stage(c):
        if c == 0:
            own_x.wait()
        for q in range(max(1, c * size), (c + 1) * size):
            send_x(q).wait_recv()
        for r in hops:
            send_p(c, r).start()
        keep_p(c).start()
        give_p(c).start()
        if c == 0:
            loads[0].wait()
            loads[1].wait()
        here = slice(c * part, (c + 1) * part)

        @pl.loop(0, n_w)
        def _(i):
            cols = pl.ds(pl.multiple_of(i * wide, wide), wide)
            av[:, cols] = jnp.dot(rx2[here, :], wg[:, cols], preferred_element_type=F32)
            bv[:, cols] = jnp.dot(rx2[here, :], wu[:, cols], preferred_element_type=F32)

    def hidden_stage(c):
        if c == 0:
            own_y.wait()
            loads[2].wait()
        for q in range(max(1, c * size), (c + 1) * size):
            send_y(q).wait_recv()
        here = slice(c * part, (c + 1) * part)
        if c == 0:
            for q in range(1, n_ex):
                send_t(q).wait_recv()
            slot_here = lax.broadcasted_iota(jnp.int32, (cap, tok), 0).astype(F32)
            slot_here = slot_here + (me_e * cap).astype(F32)
            for q in range(n_ex):
                z, x = source(q)
                note = tgt[z * n_x + x]
                fit = jnp.where(slot_here == note[0:1, :], note[2:3, :], 0.0)
                fit = fit + jnp.where(slot_here == note[1:2, :], note[3:4, :], 0.0)
                fit = jnp.sum(fit, axis=1, keepdims=True)
                wrow[q * cap : (q + 1) * cap, :] = jnp.broadcast_to(fit, (cap, LANES))
        score[...] = jnp.zeros_like(score)

        @pl.loop(0, n_w)
        def _(k):
            cols = pl.ds(pl.multiple_of(k * wide, wide), wide)
            back = dot_nt(ry2[here, :], wd[cols, :])
            a = av[:, cols]
            b = bv[:, cols]
            w = jnp.tile(wrow[here, :], (1, wide // LANES))
            sig = jax.nn.sigmoid(a)
            silu = a * sig
            hidden = (silu * b).astype(BF)
            piece = back * hidden.astype(F32)
            total = piece[:, :LANES]
            for n in range(1, wide // LANES):
                total = total + piece[:, n * LANES : (n + 1) * LANES]
            score[...] += total
            grad = back * w
            d2[c, 0, :, cols] = (grad * b * sig * (1.0 + a * (1.0 - sig))).astype(BF)
            d2[c, 1, :, cols] = (grad * silu).astype(BF)

        for copy in all_d(c):
            copy.start()
        keep_d(c).start()
        ssend2[here, :] = jnp.broadcast_to(
            jnp.sum(score[...], axis=1, keepdims=True), (part, LANES)
        ).astype(BF)
        for q in range(max(1, c * size), (c + 1) * size):
            send_c(q).start()
        if c == 0:
            own_c.start()

    def send_c(q):
        z, x = source(q)
        return copy_to(
            ssend.at[slab(q)], sret.at[slab(me_e)], csend.at[q], crecv.at[q], me_d, z * n_x + x
        )

    own_c = pltpu.make_async_copy(ssend.at[slab(0)], sret.at[slab(me_e)], lsem.at[4])

    def landing(c):
        return rr.at[:, (pos_z + c // 2) % 2, :, (pos_x + c % 2) % 2, me_e]

    def send_r(c, q):
        return copy_to(
            rg.at[c, q],
            landing(c),
            rsend.at[c * n_ex + q],
            rrecv.at[c * n_ex + q],
            me_d,
            to(q),
        )

    def keep_r(c):
        return pltpu.make_async_copy(rg.at[c, 0], landing(c), lsem.at[9 + c])

    def row_stage(c):
        for q in list(range(1, n_ex)) + [0]:
            span = pl.ds(pl.multiple_of(to(q) * feat, 16), feat)
            grad = (dot_nt(d2[c, 0], wg[span, :]) + dot_nt(d2[c, 1], wu[span, :])).astype(BF)
            for n in range(size):
                z, x = source(c * size + n)
                rg[c, q, z // 2, x // 2] = grad[n * cap : (n + 1) * cap, :].reshape(eights, 8, feat)
            if q:
                send_r(c, q).start()
            else:
                keep_r(c).start()

    def relay_stage(c):
        for r in hops:
            relay_p(c, r).wait_recv()
            relay_p(c, r).start()

    def transpose_stage(c):
        keep_p(c).wait()

        @pl.loop(0, n_y)
        def _(r):
            g = ((pos_y + r) % n_y) * 2 + 1 - core
            here = xg.at[c, group8(g)]
            copy_to(here, here, qsend.at[0], precv.at[c * n_dp + g], other, me_e).wait_recv()

        base = c * n_dp * part
        for m in range(deep // LANES):
            xtt[m * LANES : (m + 1) * LANES, :] = xg2[
                base : base + n_dp * part, m * LANES : (m + 1) * LANES
            ].T

    def gathered(c):
        keep_d(c).wait()
        arrived_d(c, other)
        for r in range(1, n_y):
            for side in range(2):
                g = ((pos_y + r) % n_y) * 2 + side
                if far and r in near:
                    @pl.when(core == (0 if r == 1 else 1))
                    def _():
                        arrived_d(c, g)

                else:
                    arrived_d(c, g)

    def weigh(c):
        transpose_stage(c)
        gathered(c)

        @pl.loop(0, n_w)
        def _(i):
            cols = pl.ds(pl.multiple_of(i * wide, wide), wide)
            total = jnp.dot(xtt[...], dg[c, :, cols], preferred_element_type=F32)
            if c:
                total = total + acc[:, cols]
            if c < CHUNKS - 1:
                acc[:, cols] = total
            else:
                total = (total * (1.0 / n_dp)).astype(BF)
                wo[0, :, cols] = total[:half]
                wo[1, :, cols] = total[half:]

                @pl.when(core == 0)
                def _():
                    own_half(i, gg_hbm).start()
                    other_half(i, gg_hbm).start()

                @pl.when(core == 1)
                def _():
                    own_half(i, gu_hbm).start()
                    other_half(i, gu_hbm).start()

    def own_half(i, out):
        cols = pl.ds(pl.multiple_of(i * wide, wide), wide)
        return pltpu.make_async_copy(wo.at[core, :, cols], out.at[:, cols], oloc.at[i])

    def other_half(i, out):
        cols = pl.ds(pl.multiple_of(i * wide, wide), wide)
        return copy_to(
            wo.at[1 - core, :, cols],
            out.at[:, cols],
            osend.at[i],
            orecv.at[i],
            other,
            me_e,
        )

    for c in range(CHUNKS):
        forward_stage(c)
        hidden_stage(c)
        if c:
            pass_on(c - 1)
        row_stage(c)
        if c:
            relay_stage(c - 1)
        if c > 1:
            weigh(c - 2)
    weigh(CHUNKS - 2)
    relay_stage(CHUNKS - 1)
    pass_on(CHUNKS - 1)
    weigh(CHUNKS - 1)

    for c in range(CHUNKS):
        keep_r(c).wait()
        for q in range(1, n_ex):
            send_r(c, q).wait_recv()

    for s in range(n_ex):
        note = tgt[s]
        choose = ((slot_no == note[0:1, :]) | (slot_no == note[1:2, :])).astype(F32).astype(BF)
        gt_ref[:, s * tok : (s + 1) * tok] = lax.dot_general(
            rr2[s], choose, (((0,), (0,)), ((), ())), preferred_element_type=F32
        ).astype(BF)

    own_c.wait()
    for q in range(1, n_ex):
        send_c(q).wait_recv()
    back_scores = sret2[...].astype(F32)
    note = tgt[me_e]
    for k in range(2):
        found = jnp.where(slot_no == note[k : k + 1, :], back_scores, 0.0)
        gs_ref[k : k + 1, :] = jnp.sum(found, axis=0, keepdims=True).astype(BF)

    for q in range(1, n_ex):
        send_t(q).wait_send()
        send_x(q).wait_send()
        send_y(q).wait_send()
        send_c(q).wait_send()
        for c in range(CHUNKS):
            send_r(c, q).wait_send()
    for c in range(CHUNKS):
        give_p(c).wait_send()
        for r in hops:
            send_p(c, r).wait_send()
            relay_p(c, r).wait_send()
        for copy in all_d(c):
            copy.wait_send()
        if far:
            for side in range(2):
                forward(c, side).wait_send()

    @pl.loop(0, n_w)
    def _(i):
        own_half(i, gg_hbm).wait()
        other_half(i, gg_hbm).wait()


def local(tokens, cotangent, gates, expert_ids, gate_w, up_w, down_w):
    tok, width = tokens.shape
    top = expert_ids.shape[1]
    n_ex = lax.axis_size("expert")
    n_dp = lax.axis_size("dp")
    cap = 3 * tok * top // (2 * n_ex)
    hid = gate_w.shape[2]
    rows = n_ex * cap
    feat = width // n_ex
    n_y = n_dp // 2
    deep = width // n_y
    n_w = hid // min(256, hid)
    vmem = pl.BlockSpec(memory_space=pltpu.VMEM)
    hbm = pl.BlockSpec(memory_space=pl.ANY)
    dma = pltpu.SemaphoreType.DMA
    part = rows // CHUNKS
    n_z, n_x = grid_of(n_ex)
    scratch = [
        pltpu.VMEM((width, hid), BF),
        pltpu.VMEM((width, hid), BF),
        pltpu.VMEM((hid, width), BF),
        pltpu.VMEM((tok, width), BF),
        pltpu.VMEM((n_ex, 8, tok), F32),
        pltpu.VMEM((rows // 8, 8, width), BF),
        pltpu.VMEM((rows // 8, 8, width), BF),
        pltpu.VMEM((rows // 8, 8, width), BF),
        pltpu.VMEM((rows // 8, 8, width), BF),
        pltpu.VMEM((part, hid), F32),
        pltpu.VMEM((part, hid), F32),
        pltpu.VMEM((CHUNKS, 2, part, hid), BF),
        pltpu.VMEM((part, LANES), F32),
        pltpu.VMEM((rows, LANES), F32),
        pltpu.VMEM((rows // 8, 8, LANES), BF),
        pltpu.VMEM((rows // 8, 8, LANES), BF),
        pltpu.VMEM((CHUNKS, n_ex, n_z // 2, n_x // 2, cap // 8, 8, feat), BF),
        pltpu.VMEM((n_z // 2, 2, n_x // 2, 2, n_ex, cap // 8, 8, feat), BF),
        pltpu.VMEM((CHUNKS, n_dp * part // 8, 8, deep), BF),
        pltpu.VMEM((CHUNKS, n_dp * part, hid), BF),
        pltpu.VMEM((deep, n_dp * part), BF),
        pltpu.VMEM((deep, hid), F32),
        pltpu.VMEM((2, deep // 2, hid), BF),
        dma((3,)),
        dma((n_ex,)),
        dma((n_ex,)),
        dma((n_ex,)),
        dma((n_ex,)),
        dma((n_ex,)),
        dma((n_ex,)),
        dma((CHUNKS * n_y,)),
        dma((CHUNKS * n_dp,)),
        dma((CHUNKS * n_y,)),
        dma((2 * CHUNKS * n_y,)),
        dma((CHUNKS * n_dp,)),
        dma((2 * CHUNKS,)),
        dma((CHUNKS,)),
        dma((CHUNKS * n_ex,)),
        dma((CHUNKS * n_ex,)),
        dma((n_ex,)),
        dma((n_ex,)),
        dma((n_w,)),
        dma((n_w,)),
        dma((n_w,)),
        dma((9 + CHUNKS,)),
    ]
    return pl.pallas_call(
        functools.partial(kernel, n_dp, n_ex, cap),
        out_shape=(
            jax.ShapeDtypeStruct((feat, n_ex * tok), BF),
            jax.ShapeDtypeStruct((width // n_dp, hid), BF),
            jax.ShapeDtypeStruct((width // n_dp, hid), BF),
            jax.ShapeDtypeStruct((top, tok), BF),
        ),
        in_specs=[vmem, vmem, hbm, hbm, hbm, hbm, hbm],
        out_specs=(vmem, hbm, hbm, vmem),
        scratch_shapes=scratch,
        compiler_params=pltpu.CompilerParams(
            collective_id=0, has_side_effects=True, vmem_limit_bytes=64 * 1024 * 1024
        ),
    )(
        expert_ids.T,
        gates.T,
        tokens,
        cotangent,
        gate_w[0],
        up_w[0],
        down_w[0],
    )


def settle(*refs):
    sources, results, held, sems = refs[:4], refs[4:8], refs[8:12], refs[12]
    pieces = []
    for k in range(4):
        count = sources[k].shape[0]
        cut = count // 2 if count % 32 == 0 else count
        pieces += [(k, pl.ds(n, cut)) for n in range(0, count, cut)]
    arrive = [
        pltpu.make_async_copy(sources[k].at[span], held[k].at[span], sems.at[0, n])
        for n, (k, span) in enumerate(pieces)
    ]
    depart = [
        pltpu.make_async_copy(held[k].at[span], results[k].at[span], sems.at[1, n])
        for n, (k, span) in enumerate(pieces)
    ]
    for copy in arrive:
        copy.start()
    for before, after in zip(arrive, depart):
        before.wait()
        after.start()
    for copy in depart:
        copy.wait()


def shard(tokens, cotangent, gates, expert_ids, gate_w, up_w, down_w):
    results = local(tokens, cotangent, gates, expert_ids, gate_w, up_w, down_w)
    hbm = pl.BlockSpec(memory_space=pl.ANY)
    grad_tokens, grad_gate, grad_up, grad_gates = pl.pallas_call(
        settle,
        out_shape=tuple(jax.ShapeDtypeStruct(r.shape, r.dtype) for r in results),
        in_specs=[hbm] * 4,
        out_specs=(hbm,) * 4,
        scratch_shapes=[pltpu.VMEM(r.shape, r.dtype) for r in results]
        + [pltpu.SemaphoreType.DMA((2, 8))],
        compiler_params=pltpu.CompilerParams(vmem_limit_bytes=16 * 1024 * 1024),
    )(*results)
    return grad_tokens.T, grad_gate[None], grad_up[None], grad_gates.T


def solution(mesh):
    placed = (
        P(("dp", "expert"), None),
        P(("dp", "expert"), None),
        P(("dp", "expert"), None),
        P(("dp", "expert"), None),
        P("expert", None, None),
        P("expert", None, None),
        P("expert", None, None),
    )
    return jax.shard_map(
        shard,
        mesh=mesh,
        in_specs=placed,
        out_specs=(
            P("dp", "expert"),
            P("expert", "dp", None),
            P("expert", "dp", None),
            P(("dp", "expert"), None),
        ),
        check_vma=False,
    )
```

```python
import functools
import jax
import jax.numpy as jnp
from jax import lax
from jax.experimental import pallas as pl
from jax.experimental.pallas import tpu as pltpu
from jax.sharding import PartitionSpec as P

MESH = pl.DeviceIdType.MESH
BF = jnp.bfloat16
F32 = jnp.float32
LANES = 128


def grid_of(count):
    side = 1
    while side * side * 4 <= count:
        side *= 2
    return count // side, side


def dot_nt(left, right):
    return lax.dot_general(left, right, (((1,), (1,)), ((), ())), preferred_element_type=F32)


def kernel(
    n_dp,
    n_ex,
    cap,
    ids_ref,
    gts_ref,
    x_hbm,
    y_hbm,
    wg_hbm,
    wu_hbm,
    wd_hbm,
    gt_ref,
    gg_hbm,
    gu_hbm,
    gs_ref,
    wg,
    wu,
    wd,
    held,
    tgt,
    sx,
    sy,
    rx,
    ry,
    av,
    bv,
    d2,
    score,
    wrow,
    ssend,
    sret,
    rg,
    rr,
    xg,
    dg,
    xtt,
    acc,
    wo,
    wsem,
    tsend,
    trecv,
    xsend,
    xrecv,
    ysend,
    yrecv,
    psend,
    precv,
    qsend,
    dsend,
    drecv,
    fsend,
    dloc,
    rsend,
    rrecv,
    csend,
    crecv,
    osend,
    orecv,
    oloc,
    lsem,
):
    n_z, n_x = grid_of(n_ex)
    n_y = n_dp // 2
    tok, width = held.shape
    hid = wg.shape[1]
    rows = n_ex * cap
    part = rows // 2
    eights = cap // 8
    span8 = part // 8
    feat = width // n_ex
    deep = width // n_y
    half = deep // 2
    tile = hid // 2
    wide = min(256, tile)
    n_w = hid // wide
    me_e = lax.axis_index("expert")
    me_d = lax.axis_index("dp")
    pos_z, pos_x = me_e // n_x, me_e % n_x
    pos_y, core = me_d // 2, me_d % 2
    other = me_d + 1 - 2 * core
    near = sorted({1, n_y - 1})
    hops = [r for r in [n_y // 2] + near if r]
    hops = sorted(set(hops), key=hops.index)

    signs = [(a, b) for b in range(n_x) for a in range(n_z)]
    signs.sort(key=lambda t: (min(t[0], n_z - t[0]) + min(t[1], n_x - t[1]), t))
    order = [t for t in signs if t[0] % 2 == 0] + [t for t in signs if t[0] % 2 == 1]
    size = n_ex // 2

    def to(q):
        return ((pos_z + order[q][0]) % n_z) * n_x + (pos_x + order[q][1]) % n_x

    def source(q):
        return ((pos_z + n_z - order[q][0]) % n_z), (pos_x + n_x - order[q][1]) % n_x

    def copy_to(src, dst, send, recv, dp_id, ex_id):
        return pltpu.make_async_remote_copy(
            src_ref=src,
            dst_ref=dst,
            send_sem=send,
            recv_sem=recv,
            device_id=(dp_id, ex_id),
            device_id_type=MESH,
        )

    def slab(o):
        return pl.ds(o * eights, eights)

    def tiles(i):
        return slice(i * tile, (i + 1) * tile)

    sx2, rx2 = sx.reshape(rows, width), rx.reshape(rows, width)
    sy2, ry2 = sy.reshape(rows, width), ry.reshape(rows, width)
    ssend2, sret2 = ssend.reshape(rows, LANES), sret.reshape(rows, LANES)
    xg2 = xg.reshape(2 * n_dp * part, deep)
    rr2 = rr.reshape(n_ex, rows, feat)

    load_x = pltpu.make_async_copy(x_hbm, held, lsem.at[7])
    load_y = pltpu.make_async_copy(y_hbm, held, lsem.at[8])
    load_x.start()
    loads = [
        pltpu.make_async_copy(wg_hbm, wg, wsem.at[0]),
        pltpu.make_async_copy(wu_hbm, wu, wsem.at[1]),
        pltpu.make_async_copy(wd_hbm, wd, wsem.at[2]),
    ]
    barrier = pltpu.get_barrier_semaphore()

    @pl.loop(1, n_ex)
    def _(o):
        partner = ((pos_z + o // n_x) % n_z) * n_x + (pos_x + o % n_x) % n_x
        pl.semaphore_signal(barrier, inc=1, device_id=(me_d, partner), device_id_type=MESH)

    @pl.loop(1, n_dp)
    def _(o):
        pl.semaphore_signal(
            barrier, inc=1, device_id=((me_d + o) % n_dp, me_e), device_id_type=MESH
        )

    ids = ids_ref[...]
    expert_no = lax.broadcasted_iota(jnp.int32, (n_ex, tok), 0)
    named = [(expert_no == ids[k : k + 1, :]).astype(F32) for k in range(2)]
    before = (
        lax.broadcasted_iota(jnp.int32, (tok, tok), 0)
        < lax.broadcasted_iota(jnp.int32, (tok, tok), 1)
    ).astype(F32)
    count = jnp.dot(
        (named[0] + named[1]).astype(BF), before.astype(BF), preferred_element_type=F32
    )
    place = [
        jnp.sum(named[k] * count, axis=0, keepdims=True) + (ids[k : k + 1, :] * cap).astype(F32)
        for k in range(2)
    ]
    slot_no = lax.broadcasted_iota(jnp.int32, (rows, tok), 0).astype(F32)
    picks = [(slot_no == place[k]).astype(F32) for k in range(2)]
    pick = (picks[0] + picks[1]).astype(BF)
    gts = gts_ref[...].astype(F32)
    tgt[me_e, 0:2, :] = jnp.concatenate(place, axis=0)
    tgt[me_e, 2:4, :] = gts
    tgt[me_e, 4:8, :] = jnp.zeros((4, tok), F32)

    def send_x(q):
        e = to(q)
        return copy_to(sx.at[slab(e)], rx.at[slab(q)], xsend.at[q], xrecv.at[q], me_d, e)

    def send_y(q):
        e = to(q)
        return copy_to(sy.at[slab(e)], ry.at[slab(q)], ysend.at[q], yrecv.at[q], me_d, e)

    def leave(src, dst, send, recv, chosen):
        for n in range(eights):
            for q in chosen:
                e = to(q)
                copy_to(
                    src.at[e * eights + n], dst.at[q * eights + n], send.at[q], recv.at[q], me_d, e
                ).start()

    def send_t(q):
        return copy_to(tgt.at[me_e], tgt.at[me_e], tsend.at[q], trecv.at[q], me_d, to(q))

    block = min(512, width)
    load_x.wait()
    for i in range(width // block):
        span = slice(i * block, (i + 1) * block)
        sx2[:, span] = jnp.dot(pick, held[:, span], preferred_element_type=F32).astype(BF)

    load_y.start()
    pl.semaphore_wait(barrier, n_ex - 1 + n_dp - 1)
    for q in range(1, n_ex):
        send_t(q).start()
    leave(sx, rx, xsend, xrecv, range(1, size))
    own_x = pltpu.make_async_copy(sx.at[slab(me_e)], rx.at[slab(0)], lsem.at[0])
    own_x.start()
    load_y.wait()
    for load in loads:
        load.start()
    for i in range(width // block):
        span = slice(i * block, (i + 1) * block)
        sy2[:, span] = jnp.dot(pick, held[:, span], preferred_element_type=F32).astype(BF)
    leave(sy, ry, ysend, yrecv, range(1, size))
    own_y = pltpu.make_async_copy(sy.at[slab(me_e)], ry.at[slab(0)], lsem.at[1])
    own_y.start()
    leave(sx, rx, xsend, xrecv, range(size, n_ex))
    leave(sy, ry, ysend, yrecv, range(size, n_ex))

    def features(chip):
        return pl.ds(pl.multiple_of(chip * deep, LANES), deep)

    def group8(g):
        return pl.ds(g * span8, span8)

    def send_p(c, r):
        chip = (pos_y + r) % n_y
        return copy_to(
            rx.at[c * span8 : (c + 1) * span8, :, features(chip)],
            xg.at[c, group8(me_d)],
            psend.at[c * n_y + r],
            precv.at[c * n_dp + me_d],
            chip * 2 + core,
            me_e,
        )

    def keep_p(c):
        return pltpu.make_async_copy(
            rx.at[c * span8 : (c + 1) * span8, :, features(pos_y)],
            xg.at[c, group8(me_d)],
            lsem.at[2 + c],
        )

    def give_p(c):
        return copy_to(
            rx.at[c * span8 : (c + 1) * span8, :, features(pos_y)],
            xg.at[c, group8(me_d)],
            qsend.at[c * n_y],
            precv.at[c * n_dp + me_d],
            other,
            me_e,
        )

    def relay_p(c, r):
        g = ((pos_y + n_y - r) % n_y) * 2 + core
        return copy_to(
            xg.at[c, group8(g)],
            xg.at[c, group8(g)],
            qsend.at[c * n_y + r],
            precv.at[c * n_dp + g],
            other,
            me_e,
        )

    def group(g):
        return pl.ds(pl.multiple_of(g * part, 16), part)

    def send_d(c, i, r, which):
        side = core if which == 0 else 1 - core
        chip = (pos_y + r) % n_y
        return copy_to(
            d2.at[c, side, :, tiles(i)],
            dg.at[c, group(me_d), tiles(i)],
            dsend.at[((c * 2 + i) * n_y + r) * 2 + which],
            drecv.at[(c * 2 + i) * n_dp + me_d],
            chip * 2 + side,
            me_e,
        )

    def keep_d(c, i):
        return pltpu.make_async_copy(
            d2.at[c, core, :, tiles(i)], dg.at[c, group(me_d), tiles(i)], dloc.at[c * 2 + i]
        )

    def all_d(c, i):
        return [send_d(c, i, r, which) for r in near for which in (0, 1)] + [send_d(c, i, 0, 1)]

    def forward(c, i, side):
        origin = (pos_y + n_y - 1 + 2 * core) % n_y
        g = origin * 2 + side
        return copy_to(
            dg.at[c, group(g), tiles(i)],
            dg.at[c, group(g), tiles(i)],
            fsend.at[(c * 2 + i) * 2 + side],
            drecv.at[(c * 2 + i) * n_dp + g],
            ((pos_y + n_y + 1 - 2 * core) % n_y) * 2 + core,
            me_e,
        )

    def arrived_d(c, i, g):
        here = dg.at[c, group(g), tiles(i)]
        copy_to(here, here, fsend.at[0], drecv.at[(c * 2 + i) * n_dp + g], other, me_e).wait_recv()

    far = n_y > 2

    def pass_on(c):
        if far:
            for i in range(2):
                for side in range(2):
                    forward(c, i, side).wait_recv()
                    forward(c, i, side).start()

    def forward_stage(c):
        if c == 0:
            own_x.wait()
        for q in range(max(1, c * size), (c + 1) * size):
            send_x(q).wait_recv()
        for r in hops:
            send_p(c, r).start()
        keep_p(c).start()
        give_p(c).start()
        if c == 0:
            loads[0].wait()
            loads[1].wait()
        here = slice(c * part, (c + 1) * part)

        @pl.loop(0, n_w)
        def _(i):
            cols = pl.ds(pl.multiple_of(i * wide, wide), wide)
            av[:, cols] = jnp.dot(rx2[here, :], wg[:, cols], preferred_element_type=F32)
            bv[:, cols] = jnp.dot(rx2[here, :], wu[:, cols], preferred_element_type=F32)

    def hidden_stage(c):
        if c == 0:
            own_y.wait()
            loads[2].wait()
        for q in range(max(1, c * size), (c + 1) * size):
            send_y(q).wait_recv()
        here = slice(c * part, (c + 1) * part)
        if c == 0:
            for q in range(1, n_ex):
                send_t(q).wait_recv()
            slot_here = lax.broadcasted_iota(jnp.int32, (cap, tok), 0).astype(F32)
            slot_here = slot_here + (me_e * cap).astype(F32)
            for q in range(n_ex):
                z, x = source(q)
                note = tgt[z * n_x + x]
                fit = jnp.where(slot_here == note[0:1, :], note[2:3, :], 0.0)
                fit = fit + jnp.where(slot_here == note[1:2, :], note[3:4, :], 0.0)
                fit = jnp.sum(fit, axis=1, keepdims=True)
                wrow[q * cap : (q + 1) * cap, :] = jnp.broadcast_to(fit, (cap, LANES))
        score[...] = jnp.zeros_like(score)
        for i in range(2):

            @pl.loop(0, tile // wide)
            def _(k):
                cols = pl.ds(pl.multiple_of(i * tile + k * wide, wide), wide)
                back = dot_nt(ry2[here, :], wd[cols, :])
                a = av[:, cols]
                b = bv[:, cols]
                w = jnp.tile(wrow[here, :], (1, wide // LANES))
                sig = jax.nn.sigmoid(a)
                silu = a * sig
                hidden = (silu * b).astype(BF)
                piece = back * hidden.astype(F32)
                total = piece[:, :LANES]
                for n in range(1, wide // LANES):
                    total = total + piece[:, n * LANES : (n + 1) * LANES]
                score[...] += total
                grad = back * w
                d2[c, 0, :, cols] = (grad * b * sig * (1.0 + a * (1.0 - sig))).astype(BF)
                d2[c, 1, :, cols] = (grad * silu).astype(BF)

            for copy in all_d(c, i):
                copy.start()
            keep_d(c, i).start()
        ssend2[here, :] = jnp.broadcast_to(
            jnp.sum(score[...], axis=1, keepdims=True), (part, LANES)
        ).astype(BF)
        for q in range(max(1, c * size), (c + 1) * size):
            send_c(q).start()
        if c == 0:
            own_c.start()

    def send_c(q):
        z, x = source(q)
        return copy_to(
            ssend.at[slab(q)], sret.at[slab(me_e)], csend.at[q], crecv.at[q], me_d, z * n_x + x
        )

    own_c = pltpu.make_async_copy(ssend.at[slab(0)], sret.at[slab(me_e)], lsem.at[4])

    def landing(c):
        return rr.at[:, (pos_z + c) % 2, :, me_e]

    def send_r(c, q):
        return copy_to(
            rg.at[c, q],
            landing(c),
            rsend.at[c * n_ex + q],
            rrecv.at[c * n_ex + q],
            me_d,
            to(q),
        )

    def keep_r(c):
        return pltpu.make_async_copy(rg.at[c, 0], landing(c), lsem.at[5 + c])

    def row_stage(c):
        for q in list(range(1, n_ex)) + [0]:
            span = pl.ds(pl.multiple_of(to(q) * feat, 16), feat)
            grad = (dot_nt(d2[c, 0], wg[span, :]) + dot_nt(d2[c, 1], wu[span, :])).astype(BF)
            for n in range(size):
                z, x = source(c * size + n)
                rg[c, q, z // 2, x] = grad[n * cap : (n + 1) * cap, :].reshape(eights, 8, feat)
            if q:
                send_r(c, q).start()
            else:
                keep_r(c).start()

    def relay_stage(c):
        for r in hops:
            relay_p(c, r).wait_recv()
            relay_p(c, r).start()

    def transpose_stage(c):
        keep_p(c).wait()

        @pl.loop(0, n_y)
        def _(r):
            g = ((pos_y + r) % n_y) * 2 + 1 - core
            here = xg.at[c, group8(g)]
            copy_to(here, here, qsend.at[0], precv.at[c * n_dp + g], other, me_e).wait_recv()

        base = c * n_dp * part
        for m in range(deep // LANES):
            xtt[m * LANES : (m + 1) * LANES, :] = xg2[
                base : base + n_dp * part, m * LANES : (m + 1) * LANES
            ].T

    def gathered(c, i):
        keep_d(c, i).wait()
        arrived_d(c, i, other)
        for r in range(1, n_y):
            chip = (pos_y + r) % n_y

            for side in range(2):
                g = chip * 2 + side
                if far and r == 1:
                    @pl.when(core == 0)
                    def _():
                        arrived_d(c, i, g)

                elif far and r == n_y - 1:

                    @pl.when(core == 1)
                    def _():
                        arrived_d(c, i, g)

                else:
                    arrived_d(c, i, g)

    def own_half(i, out):
        cols = pl.ds(pl.multiple_of(i * wide, wide), wide)
        return pltpu.make_async_copy(wo.at[core, :, cols], out.at[:, cols], oloc.at[i])

    def other_half(i, out):
        cols = pl.ds(pl.multiple_of(i * wide, wide), wide)
        return copy_to(
            wo.at[1 - core, :, cols],
            out.at[:, cols],
            osend.at[i],
            orecv.at[i],
            other,
            me_e,
        )

    forward_stage(0)
    hidden_stage(0)
    relay_stage(0)
    row_stage(0)
    forward_stage(1)
    pass_on(0)
    hidden_stage(1)
    relay_stage(1)
    row_stage(1)

    transpose_stage(0)
    for i in range(2):
        gathered(0, i)

    @pl.loop(0, n_w)
    def _(i):
        cols = pl.ds(pl.multiple_of(i * wide, wide), wide)
        acc[:, cols] = jnp.dot(xtt[...], dg[0, :, cols], preferred_element_type=F32)

    pass_on(1)
    transpose_stage(1)

    for c in range(2):
        keep_r(c).wait()
        for q in range(1, n_ex):
            send_r(c, q).wait_recv()

    for s in range(n_ex):
        z, x = s // n_x, s % n_x
        note = tgt[s]
        choose = ((slot_no == note[0:1, :]) | (slot_no == note[1:2, :])).astype(F32).astype(BF)
        place_no = ((z // 2) * 2 + z % 2) * n_x + x
        gt_ref[:, s * tok : (s + 1) * tok] = lax.dot_general(
            rr2[place_no], choose, (((0,), (0,)), ((), ())), preferred_element_type=F32
        ).astype(BF)

    for k in range(2):
        gathered(1, k)

        @pl.loop(k * (n_w // 2), (k + 1) * (n_w // 2))
        def _(i):
            cols = pl.ds(pl.multiple_of(i * wide, wide), wide)
            total = acc[:, cols] + jnp.dot(xtt[...], dg[1, :, cols], preferred_element_type=F32)
            total = (total * (1.0 / n_dp)).astype(BF)
            wo[0, :, cols] = total[:half]
            wo[1, :, cols] = total[half:]

            @pl.when(core == 0)
            def _():
                own_half(i, gg_hbm).start()
                other_half(i, gg_hbm).start()

            @pl.when(core == 1)
            def _():
                own_half(i, gu_hbm).start()
                other_half(i, gu_hbm).start()

    own_c.wait()
    for q in range(1, n_ex):
        send_c(q).wait_recv()
    back_scores = sret2[...].astype(F32)
    note = tgt[me_e]
    for k in range(2):
        found = jnp.where(slot_no == note[k : k + 1, :], back_scores, 0.0)
        gs_ref[k : k + 1, :] = jnp.sum(found, axis=0, keepdims=True).astype(BF)

    for q in range(1, n_ex):
        send_t(q).wait_send()
        send_x(q).wait_send()
        send_y(q).wait_send()
        send_c(q).wait_send()
        for c in range(2):
            send_r(c, q).wait_send()
    for c in range(2):
        give_p(c).wait_send()
        for r in hops:
            send_p(c, r).wait_send()
            relay_p(c, r).wait_send()
        for i in range(2):
            for copy in all_d(c, i):
                copy.wait_send()
            if far:
                for side in range(2):
                    forward(c, i, side).wait_send()

    @pl.loop(0, n_w)
    def _(i):
        own_half(i, gg_hbm).wait()
        other_half(i, gg_hbm).wait()


def local(tokens, cotangent, gates, expert_ids, gate_w, up_w, down_w):
    tok, width = tokens.shape
    top = expert_ids.shape[1]
    n_ex = lax.axis_size("expert")
    n_dp = lax.axis_size("dp")
    cap = 3 * tok * top // (2 * n_ex)
    hid = gate_w.shape[2]
    rows = n_ex * cap
    feat = width // n_ex
    n_y = n_dp // 2
    deep = width // n_y
    n_w = hid // min(256, hid // 2)
    vmem = pl.BlockSpec(memory_space=pltpu.VMEM)
    hbm = pl.BlockSpec(memory_space=pl.ANY)
    dma = pltpu.SemaphoreType.DMA
    part = rows // 2
    n_z, n_x = grid_of(n_ex)
    scratch = [
        pltpu.VMEM((width, hid), BF),
        pltpu.VMEM((width, hid), BF),
        pltpu.VMEM((hid, width), BF),
        pltpu.VMEM((tok, width), BF),
        pltpu.VMEM((n_ex, 8, tok), F32),
        pltpu.VMEM((rows // 8, 8, width), BF),
        pltpu.VMEM((rows // 8, 8, width), BF),
        pltpu.VMEM((rows // 8, 8, width), BF),
        pltpu.VMEM((rows // 8, 8, width), BF),
        pltpu.VMEM((part, hid), F32),
        pltpu.VMEM((part, hid), F32),
        pltpu.VMEM((2, 2, part, hid), BF),
        pltpu.VMEM((part, LANES), F32),
        pltpu.VMEM((rows, LANES), F32),
        pltpu.VMEM((rows // 8, 8, LANES), BF),
        pltpu.VMEM((rows // 8, 8, LANES), BF),
        pltpu.VMEM((2, n_ex, n_z // 2, n_x, cap // 8, 8, feat), BF),
        pltpu.VMEM((n_z // 2, 2, n_x, n_ex, cap // 8, 8, feat), BF),
        pltpu.VMEM((2, n_dp * part // 8, 8, deep), BF),
        pltpu.VMEM((2, n_dp * part, hid), BF),
        pltpu.VMEM((deep, n_dp * part), BF),
        pltpu.VMEM((deep, hid), F32),
        pltpu.VMEM((2, deep // 2, hid), BF),
        dma((3,)),
        dma((n_ex,)),
        dma((n_ex,)),
        dma((n_ex,)),
        dma((n_ex,)),
        dma((n_ex,)),
        dma((n_ex,)),
        dma((2 * n_y,)),
        dma((2 * n_dp,)),
        dma((2 * n_y,)),
        dma((8 * n_y,)),
        dma((4 * n_dp,)),
        dma((8,)),
        dma((4,)),
        dma((2 * n_ex,)),
        dma((2 * n_ex,)),
        dma((n_ex,)),
        dma((n_ex,)),
        dma((n_w,)),
        dma((n_w,)),
        dma((n_w,)),
        dma((9,)),
    ]
    return pl.pallas_call(
        functools.partial(kernel, n_dp, n_ex, cap),
        out_shape=(
            jax.ShapeDtypeStruct((feat, n_ex * tok), BF),
            jax.ShapeDtypeStruct((width // n_dp, hid), BF),
            jax.ShapeDtypeStruct((width // n_dp, hid), BF),
            jax.ShapeDtypeStruct((top, tok), BF),
        ),
        in_specs=[vmem, vmem, hbm, hbm, hbm, hbm, hbm],
        out_specs=(vmem, hbm, hbm, vmem),
        scratch_shapes=scratch,
        compiler_params=pltpu.CompilerParams(
            collective_id=0, has_side_effects=True, vmem_limit_bytes=64 * 1024 * 1024
        ),
    )(
        expert_ids.T,
        gates.T,
        tokens,
        cotangent,
        gate_w[0],
        up_w[0],
        down_w[0],
    )


def settle(*refs):
    sources, results, held, sems = refs[:4], refs[4:8], refs[8:12], refs[12]
    pieces = []
    for k in range(4):
        count = sources[k].shape[0]
        cut = count // 2 if count % 32 == 0 else count
        pieces += [(k, pl.ds(n, cut)) for n in range(0, count, cut)]
    arrive = [
        pltpu.make_async_copy(sources[k].at[span], held[k].at[span], sems.at[0, n])
        for n, (k, span) in enumerate(pieces)
    ]
    depart = [
        pltpu.make_async_copy(held[k].at[span], results[k].at[span], sems.at[1, n])
        for n, (k, span) in enumerate(pieces)
    ]
    for copy in arrive:
        copy.start()
    for before, after in zip(arrive, depart):
        before.wait()
        after.start()
    for copy in depart:
        copy.wait()


def shard(tokens, cotangent, gates, expert_ids, gate_w, up_w, down_w):
    results = local(tokens, cotangent, gates, expert_ids, gate_w, up_w, down_w)
    hbm = pl.BlockSpec(memory_space=pltpu.HBM)
    grad_tokens, grad_gate, grad_up, grad_gates = pl.pallas_call(
        settle,
        out_shape=tuple(jax.ShapeDtypeStruct(r.shape, r.dtype) for r in results),
        in_specs=[hbm] * 4,
        out_specs=(hbm,) * 4,
        scratch_shapes=[pltpu.VMEM(r.shape, r.dtype) for r in results]
        + [pltpu.SemaphoreType.DMA((2, 8))],
        compiler_params=pltpu.CompilerParams(vmem_limit_bytes=16 * 1024 * 1024),
    )(*results)
    return grad_tokens.T, grad_gate[None], grad_up[None], grad_gates.T


def solution(mesh):
    placed = (
        P(("dp", "expert"), None),
        P(("dp", "expert"), None),
        P(("dp", "expert"), None),
        P(("dp", "expert"), None),
        P("expert", None, None),
        P("expert", None, None),
        P("expert", None, None),
    )
    return jax.shard_map(
        shard,
        mesh=mesh,
        in_specs=placed,
        out_specs=(
            P("dp", "expert"),
            P("expert", "dp", None),
            P("expert", "dp", None),
            P(("dp", "expert"), None),
        ),
        check_vma=False,
    )
```
